32 devices in a mesh: req: 4 (over z), seq: 8 (over y, x, core).
Axes of the slice: x: 2, y: 2, z: 4, core: 2. Of those that a mesh axis runs over, the one named last changes fastest.
Arguments:
- hidden_in: bfloat16 [4, 32, 4, 2048], P(None, 'req', None, 'seq'), may hold values from -30 to 30
- cache_lens: int32 [32], P('req'), may hold values from 1 to 4092, as said below
- page_table: int32 [32, 32], P('req'), may hold values from -1 to 55, as said below
- key_cache: bfloat16 [224, 128, 1024], P(('req', 'seq')), may hold values from -250 to 250
- value_cache: bfloat16 [224, 128, 1024], P(('req', 'seq')), may hold values from -4 to 4
- norm_attn: float32 [8192], replicated, may hold values from 0.1 to 1.9
- w_qkv: bfloat16 [8192, 10240], P(None, 'seq'), may hold values from -0.0625 to 0.0625
- b_qkv: bfloat16 [10240], P('seq'), may hold values from -3 to 3
- w_out: bfloat16 [8192, 4, 2048], P(None, None, 'seq'), may hold values from -0.25 to 0.25
- norm_mlp: float32 [8192], replicated, may hold values from 0.1 to 1.9
- w_gate: bfloat16 [8192, 29568], P('req', 'seq'), may hold values from -0.0625 to 0.0625
- w_up: bfloat16 [8192, 29568], P('req', 'seq'), may hold values from -0.0625 to 0.0625
- w_down: bfloat16 [29568, 8192], P('seq', 'req'), may hold values from -0.03125 to 0.03125
Outputs:
- hidden_out: bfloat16 [4, 32, 4, 2048], P(None, 'req', None, 'seq')
- key_cache_out: bfloat16 [224, 128, 1024], P(('req', 'seq'))
- value_cache_out: bfloat16 [224, 128, 1024], P(('req', 'seq'))
The draws below stay inside these ranges and needn't reach their ends.
Inputs may be any that keep to these rules, and one draw needn't show every extreme that they name: `cache_lens`: in each group of 8 requests exactly one holds 4092 tokens and one holds 380; every other one holds at most 380. For request r and logical page j below ceil((cache_lens[r]+4)/128), page_table[r, j] is a slot of the group's 56 page slots (slot s*7+p is the p-th slot of seq index s); no slot is named twice within a group; all other entries are -1.
All inputs are finite; a program needn't handle non-finite values.
Results may differ from the reference program's by a relative error of at most 0.012.
The reference program's roundings to bfloat16 on the way count: a program that leaves them out, or rounds other values in their place, can miss the bound.
Values may be sent and summed in bfloat16 or wider, within the bound.
A program may use at most 320 MiB of HBM per device.

```python
import math
import jax
import jax.numpy as jnp
from jax import lax

D = 8192
H = 64
KV = 8
HD = 128
FF = 29568
STEPS = 4
PAGE = 128
PMAX = 32
RG = 8
GROUPS = 4
R = 32
WIDTH_PART = 2048
QKVW = 10240
POOL = 56
NPAGES = 224
LONGEST = 4096
SHORT_PAGES = 3


def plan_group(key):
    keys = jax.random.split(key, 4)
    short_top = SHORT_PAGES * PAGE - STEPS
    first = jax.random.randint(keys[0], (RG,), 0, short_top)
    second = jax.random.randint(keys[1], (RG,), 0, short_top)
    lengths = 1 + first * second // short_top
    longest = jax.random.randint(keys[2], (), 0, RG)
    index = jnp.arange(RG)
    lengths = jnp.where(index == longest, LONGEST - STEPS, jnp.where(index == (longest + 1) % RG, short_top, lengths))
    pages = (lengths + STEPS + PAGE - 1) // PAGE
    order = jax.random.permutation(keys[3], POOL)
    order = jnp.where(order == POOL - 1, order[0], order).at[0].set(POOL - 1)
    starts = jnp.cumsum(pages) - pages
    column = jnp.arange(PMAX)
    entry = order[jnp.clip(starts[:, None] + column[None, :], 0, POOL - 1)]
    table = jnp.where(column[None, :] < pages[:, None], entry, -1)
    return (lengths.astype(jnp.int32), table.astype(jnp.int32))


def plan_all(key):
    keys = jax.random.split(jax.random.fold_in(key, 11), R // RG)
    return jax.vmap(plan_group)(keys)


def draw_cache_lens(key, part):
    lengths, table = plan_all(key)
    return lengths.reshape(R)


def draw_page_table(key, part):
    lengths, table = plan_all(key)
    return table.reshape(R, PMAX)


def draw_hidden_in(key, part):
    groups = R // RG
    width = D // groups
    keys = jax.random.split(key, 3)
    shape = (STEPS, R, groups, width)
    column = jnp.arange(D, dtype=jnp.float32).reshape(1, 1, groups, width) / D
    factor = jnp.exp(jax.random.uniform(keys[1], (1, 1, groups, width), minval=0.0, maxval=math.log(3.5)))
    rows = jnp.exp(jax.random.uniform(keys[2], (STEPS, R, 1, 1), minval=math.log(0.6), maxval=math.log(1.7)))
    noise = jnp.clip(jax.random.normal(keys[0], shape), -4.0, 4.0)
    ramp = 0.25 * 3.0 ** column
    return (noise * ramp * factor * rows).astype(jnp.bfloat16)


def draw_key_cache(key, part):
    shape = (NPAGES, PAGE // 2, 2, KV * HD)
    keys = jax.random.split(key, 1)
    base = jnp.clip(jax.random.normal(keys[0], shape), -4.0, 4.0)
    return base.reshape(NPAGES, PAGE, KV * HD).astype(jnp.bfloat16)


def block_levels(stream_key, dims, shards, low, top_value):
    level = 1.0
    for axis_at, blocks in shards:
        draws = jax.random.uniform(jax.random.fold_in(jax.random.fold_in(stream_key, 6), axis_at), (blocks,), jnp.float32, low / len(shards), top_value / len(shards))
        level = level * jnp.repeat(jnp.exp(draws), dims[axis_at] // blocks).reshape((-1,) + (1,) * (len(dims) - 1 - axis_at))
    return level


def scatter_about(stream_key, shape, spread, most, cuts=(), kind=jnp.bfloat16):
    values = jax.random.normal(stream_key, shape, jnp.float32) * spread
    if len(cuts) > 0:
        values = block_levels(stream_key, shape, cuts, -0.22, 0.18) * values
    return jnp.clip(values, min=-most, max=most).astype(kind)


def setup_inputs(seed: int = 0) -> dict:
    key_list = jax.random.split(jax.random.key(seed), 14)
    return {
        "hidden_in": draw_hidden_in(jax.random.fold_in(key_list[13], 71), 0),
        "cache_lens": draw_cache_lens(jax.random.fold_in(key_list[13], 71), 0),
        "page_table": draw_page_table(jax.random.fold_in(key_list[13], 71), 0),
        "key_cache": draw_key_cache(jax.random.fold_in(key_list[13], 71), 0),
        "value_cache": scatter_about(key_list[4], (NPAGES, PAGE, KV * HD), 1.0, 4.0, ((0, 32),)),
        "norm_attn": jnp.clip(1.0 + 0.18 * jax.random.normal(key_list[5], (D,), jnp.float32), 0.1, 1.9),
        "w_qkv": scatter_about(key_list[6], (D, QKVW), D ** -0.5, 0.0625, ((1, 8),)),
        "b_qkv": scatter_about(key_list[7], (QKVW,), 0.5, 3.0, ((0, 8),)),
        "w_out": scatter_about(key_list[8], (H * HD, GROUPS, WIDTH_PART), (H * HD // 16) ** -0.5, 0.25, ((2, 8),)),
        "norm_mlp": jnp.clip(1.0 + 0.18 * jax.random.normal(key_list[9], (D,), jnp.float32), 0.1, 1.9),
        "w_gate": scatter_about(key_list[10], (D, FF), D ** -0.5, 0.0625, ((0, 4), (1, 8))),
        "w_up": scatter_about(key_list[11], (D, FF), D ** -0.5, 0.0625, ((0, 4), (1, 8))),
        "w_down": scatter_about(key_list[12], (FF, D), FF ** -0.5, 0.03125, ((0, 8), (1, 4))),
    }


EPSILON = 1e-06
THETA = 1000000.0
NEGATIVE = -1e+30

def rotate(heads, position):
    half = heads.shape[-1] // 2
    freq = THETA ** (-(jnp.arange(half, dtype=jnp.float32) * 2.0 / heads.shape[-1]))
    angle = position.astype(jnp.float32)[:, None, None] * freq[None, None, :]
    cosine = jnp.cos(angle)
    sine = jnp.sin(angle)
    first = heads[..., :half]
    second = heads[..., half:]
    return jnp.concatenate([first * cosine - second * sine, second * cosine + first * sine], axis=-1)

def normalize(values, gain):
    return values * lax.rsqrt(lax.optimization_barrier(jnp.mean(values * values, axis=1, keepdims=True)) + EPSILON) * gain

def reference(hidden_in, cache_lens, page_table, key_cache, value_cache, norm_attn, w_qkv, b_qkv, w_out, norm_mlp, w_gate, w_up, w_down):
    group = H // KV
    scale = 1.0 / math.sqrt(HD)
    blocks = R // RG
    owner_group = jnp.arange(R, dtype=jnp.int32) // RG
    used = page_table >= 0
    global_pages = jnp.where(used, page_table + owner_group[:, None] * POOL, 0).astype(jnp.int32)
    offsets = jnp.arange(PMAX, dtype=jnp.int32)[:, None] * PAGE + jnp.arange(PAGE, dtype=jnp.int32)[None, :]
    w_out_flat = w_out.reshape(H * HD, D)
    outputs = []
    for step in range(STEPS):
        current = hidden_in[step].reshape(R, D).astype(jnp.float32)
        normed = normalize(current, norm_attn).astype(jnp.bfloat16)
        projected = (jnp.dot(normed, w_qkv, preferred_element_type=jnp.float32) + b_qkv.astype(jnp.float32)).astype(jnp.bfloat16)
        position = (cache_lens + step).astype(jnp.int32)
        queries = rotate(projected[:, :H * HD].reshape(R, H, HD).astype(jnp.float32), position).astype(jnp.bfloat16)
        new_keys = rotate(projected[:, H * HD:(H + KV) * HD].reshape(R, KV, HD).astype(jnp.float32), position).astype(jnp.bfloat16).reshape(R, KV * HD)
        new_values = projected[:, (H + KV) * HD:]
        target = jnp.take_along_axis(global_pages, (position // PAGE)[:, None].astype(jnp.int32), axis=1)[:, 0]
        inside = (position % PAGE).astype(jnp.int32)
        key_cache = key_cache.at[target, inside].set(new_keys)
        value_cache = value_cache.at[target, inside].set(new_values)

        def attend(inputs):
            query, pages, live, last = inputs
            keys = key_cache[pages].reshape(PMAX, PAGE, KV, HD).astype(jnp.float32)
            values = value_cache[pages].reshape(PMAX, PAGE, KV, HD).astype(jnp.float32)
            valid = jnp.logical_and(live[:, None], offsets <= last)[:, None, None, :]
            scores = jnp.einsum('kgd,jpkd->jkgp', query.reshape(KV, group, HD).astype(jnp.float32), keys, precision=lax.Precision.HIGHEST) * scale
            masked = jnp.where(valid, scores, NEGATIVE)
            page_max = lax.optimization_barrier(jnp.max(masked, axis=3))
            weights = jnp.where(valid, jnp.exp(masked - page_max[..., None]), 0.0).astype(jnp.bfloat16)
            weights = lax.optimization_barrier(weights).astype(jnp.float32)
            page_sum = lax.optimization_barrier(jnp.sum(weights, axis=3))
            page_acc = jnp.einsum('jkgp,jpkd->jkgd', weights, values, precision=lax.Precision.HIGHEST)
            top = lax.optimization_barrier(jnp.max(page_max, axis=0))
            factor = jnp.exp(page_max - top[None])
            total = lax.optimization_barrier(jnp.sum(factor * page_sum, axis=0))
            summed = lax.optimization_barrier(jnp.sum(factor[..., None] * page_acc, axis=0))
            return (summed / total[..., None]).reshape(H, HD)
        attended = lax.map(attend, (queries, global_pages, used, position)).reshape(R, H * HD).astype(jnp.bfloat16)
        middle = (current + jnp.dot(attended, w_out_flat, preferred_element_type=jnp.float32)).astype(jnp.bfloat16)
        middle_f = middle.astype(jnp.float32)
        normed_mid = normalize(middle_f, norm_mlp).astype(jnp.bfloat16)
        gate = jnp.dot(normed_mid, w_gate, preferred_element_type=jnp.float32)
        upward = jnp.dot(normed_mid, w_up, preferred_element_type=jnp.float32)
        hidden = (jax.nn.silu(gate) * upward).astype(jnp.bfloat16)
        result = (middle_f + jnp.dot(hidden, w_down, preferred_element_type=jnp.float32)).astype(jnp.bfloat16)
        outputs.append(result.reshape(R, blocks, D // blocks))
    return (jnp.stack(outputs), key_cache, value_cache)
```

```python
import math

import jax
import jax.numpy as jnp
from jax import lax
from jax.sharding import PartitionSpec as P

D = 8192
H = 64
KV = 8
HD = 128
STEPS = 4


EPSILON = 1e-06
THETA = 1000000.0
NEGATIVE = -1e30


def rotate(heads, position):
    half = heads.shape[-1] // 2
    freq = THETA ** (-(jnp.arange(half, dtype=jnp.float32) * 2.0 / heads.shape[-1]))
    angle = position.astype(jnp.float32)[:, None, None] * freq[None, None, :]
    cosine = jnp.cos(angle)
    sine = jnp.sin(angle)
    first = heads[..., :half]
    second = heads[..., half:]
    return jnp.concatenate(
        [first * cosine - second * sine, second * cosine + first * sine], axis=-1
    )


def on_device(
    hidden_in,
    cache_lens,
    page_table,
    key_cache,
    value_cache,
    norm_attn,
    w_qkv,
    b_qkv,
    w_out,
    norm_mlp,
    w_gate,
    w_up,
    w_down,
):
    steps, requests, blocks, pieces = hidden_in.shape
    rows = steps * requests
    slots, per_page, _ = key_cache.shape
    group = H // KV
    quarter = D // blocks
    seq = quarter // pieces
    scale = 1.0 / math.sqrt(HD)
    slot_ids = lax.axis_index("seq") * slots + jnp.arange(slots, dtype=jnp.int32)
    matches = page_table[:, :, None] == slot_ids[None, None, :]
    live = jnp.any(matches, axis=(0, 1))
    owner = jnp.sum(
        jnp.where(matches, jnp.arange(requests, dtype=jnp.int32)[:, None, None], 0), axis=(0, 1)
    )
    logical = jnp.sum(
        jnp.where(matches, jnp.arange(page_table.shape[1], dtype=jnp.int32)[None, :, None], 0),
        axis=(0, 1),
    )
    owned = jnp.logical_and(
        jnp.arange(requests, dtype=jnp.int32)[None, :] == owner[:, None], live[:, None]
    )
    slot_length = jnp.sum(jnp.where(owned, cache_lens[None, :], 0), axis=1)
    positions = logical[:, None] * per_page + jnp.arange(per_page, dtype=jnp.int32)[None, :]

    flat = (
        lax.all_gather(hidden_in, "seq", axis=3, tiled=True).reshape(rows, D).astype(jnp.float32)
    )
    normed = (
        flat * lax.rsqrt(jnp.mean(flat * flat, axis=1, keepdims=True) + EPSILON) * norm_attn
    ).astype(jnp.bfloat16)
    columns = (
        jnp.dot(normed, w_qkv, preferred_element_type=jnp.float32) + b_qkv.astype(jnp.float32)
    ).astype(jnp.bfloat16)
    projected = lax.all_gather(columns, "seq", axis=1, tiled=True)
    position = (
        jnp.arange(steps, dtype=jnp.int32)[:, None] + cache_lens[None, :]
    ).reshape(rows)
    rotated = rotate(
        projected[:, : (H + KV) * HD].reshape(rows, H + KV, HD).astype(jnp.float32), position
    ).astype(jnp.bfloat16)
    queries = rotated[:, :H].reshape(steps, requests, KV, group, HD)
    new_keys = rotated[:, H:].reshape(steps, requests, KV * HD)
    new_values = projected[:, (H + KV) * HD :].reshape(steps, requests, KV * HD)
    slot_keys = jnp.take(new_keys, owner, axis=1)
    slot_values = jnp.take(new_values, owner, axis=1)
    for step in range(steps):
        write_here = jnp.logical_and(live[:, None], positions == (slot_length + step)[:, None])[
            :, :, None
        ]
        key_cache = jnp.where(write_here, slot_keys[step][:, None, :], key_cache)
        value_cache = jnp.where(write_here, slot_values[step][:, None, :], value_cache)

    slot_queries = jnp.take(queries, owner, axis=1)
    keys_view = key_cache.reshape(slots, per_page, KV, HD)
    values_view = value_cache.reshape(slots, per_page, KV, HD)
    scores = (
        jnp.einsum("tjkgd,jpkd->jktgp", slot_queries, keys_view, preferred_element_type=jnp.float32)
        * scale
    )
    last = slot_length[:, None] + jnp.arange(steps, dtype=jnp.int32)[None, :]
    valid = jnp.logical_and(
        live[:, None, None], positions[:, None, :] <= last[:, :, None]
    )[:, None, :, None, :]
    masked = jnp.where(valid, scores, NEGATIVE)
    page_max = jnp.max(masked, axis=4)
    weights = jnp.where(valid, jnp.exp(masked - page_max[..., None]), 0.0).astype(jnp.bfloat16)
    page_sum = jnp.sum(weights.astype(jnp.float32), axis=4)
    page_acc = jnp.einsum(
        "jktgp,jpkd->jktgd", weights, values_view, preferred_element_type=jnp.float32
    )
    spread = owned[:, :, None, None, None]
    candidates = jnp.where(spread, page_max[:, None], NEGATIVE)
    top = jnp.max(candidates, axis=0)
    factor = jnp.where(spread, jnp.exp(candidates - top[None]), 0.0)
    total = jnp.sum(factor * page_sum[:, None], axis=0)
    summed = jnp.sum(factor[..., None] * page_acc[:, None], axis=0)
    def by_head(value):
        value = jnp.moveaxis(value, 0, 3)
        value = jnp.swapaxes(value, 1, 2)
        return value.reshape((seq, H // seq, rows) + value.shape[4:])

    packed = jnp.concatenate(
        [
            by_head(summed).reshape(seq, -1),
            by_head(top).reshape(seq, -1),
            by_head(total).reshape(seq, -1),
        ],
        axis=1,
    )
    packed = lax.all_to_all(packed, "seq", split_axis=0, concat_axis=0, tiled=True)
    count = (H // seq) * rows
    part_acc = packed[:, : count * HD].reshape(seq, count, HD)
    part_top = packed[:, count * HD : count * (HD + 1)]
    part_sum = packed[:, count * (HD + 1) :]
    best = jnp.max(part_top, axis=0)
    share = jnp.exp(part_top - best[None])
    denominator = jnp.sum(share * part_sum, axis=0)
    numerator = jnp.sum(share[..., None] * part_acc, axis=0)
    heads = (numerator / denominator[:, None]).astype(jnp.bfloat16)
    heads = jnp.swapaxes(heads.reshape(H // seq, rows, HD), 0, 1).reshape(rows, -1)
    attended = lax.all_gather(heads, "seq", axis=1, tiled=True)
    branch_out = jnp.dot(
        attended, w_out.reshape(H * HD, blocks * pieces), preferred_element_type=jnp.float32
    ).reshape(rows, blocks, pieces)
    current = hidden_in.reshape(rows, blocks, pieces).astype(jnp.float32)
    middle = (current + branch_out).astype(jnp.bfloat16)
    rows_mid = lax.all_gather(middle, "seq", axis=2, tiled=True).astype(jnp.float32)
    inverse = lax.rsqrt(jnp.mean(rows_mid * rows_mid, axis=(1, 2), keepdims=True) + EPSILON)
    normed_mid = (rows_mid * inverse * norm_mlp.reshape(blocks, quarter)).astype(jnp.bfloat16)
    mine = lax.all_to_all(normed_mid, "req", split_axis=1, concat_axis=0, tiled=True).reshape(
        -1, quarter
    )
    gate_part = jnp.dot(mine, w_gate, preferred_element_type=jnp.float32).astype(jnp.bfloat16)
    up_part = jnp.dot(mine, w_up, preferred_element_type=jnp.float32).astype(jnp.bfloat16)
    gate_sum = lax.psum_scatter(gate_part, "req", scatter_dimension=0, tiled=True)
    up_sum = lax.psum_scatter(up_part, "req", scatter_dimension=0, tiled=True)
    hidden_part = (
        jax.nn.silu(gate_sum.astype(jnp.float32)) * up_sum.astype(jnp.float32)
    ).astype(jnp.bfloat16)
    hidden = lax.all_gather(hidden_part, "req", axis=0, tiled=True)
    down = jnp.dot(hidden, w_down, preferred_element_type=jnp.float32)
    sums = lax.psum_scatter(
        down.reshape(down.shape[0], 1, quarter).astype(jnp.bfloat16),
        "seq",
        scatter_dimension=2,
        tiled=True,
    ).astype(jnp.float32)
    back = lax.all_to_all(sums, "req", split_axis=0, concat_axis=1, tiled=True)
    output = (middle.astype(jnp.float32) + back).astype(jnp.bfloat16)
    return (output.reshape(hidden_in.shape), key_cache, value_cache)


def solution(mesh):
    in_specs = (
        P(None, "req", None, "seq"),
        P("req"),
        P("req", None),
        P(("req", "seq"), None, None),
        P(("req", "seq"), None, None),
        P(),
        P(None, "seq"),
        P("seq"),
        P(None, None, "seq"),
        P(),
        P("req", "seq"),
        P("req", "seq"),
        P("seq", "req"),
    )
    out_specs = (
        P(None, "req", None, "seq"),
        P(("req", "seq"), None, None),
        P(("req", "seq"), None, None),
    )
    return jax.shard_map(
        on_device, mesh=mesh, in_specs=in_specs, out_specs=out_specs, check_vma=False
    )
```

```python
import functools
import math

import jax
import jax.numpy as jnp
from jax import lax
from jax.experimental import pallas as pl
from jax.experimental.pallas import tpu as pltpu
from jax.sharding import PartitionSpec as P

D = 8192
H = 64
KV = 8
HD = 128
STEPS = 4


EPSILON = 1e-06
THETA = 1000000.0
NEGATIVE = -1e30


def rotate(heads, position):
    half = heads.shape[-1] // 2
    freq = THETA ** (-(jnp.arange(half, dtype=jnp.float32) * 2.0 / heads.shape[-1]))
    angle = position.astype(jnp.float32)[:, None, None] * freq[None, None, :]
    cosine = jnp.cos(angle)
    sine = jnp.sin(angle)
    first = heads[..., :half]
    second = heads[..., half:]
    return jnp.concatenate(
        [first * cosine - second * sine, second * cosine + first * sine], axis=-1
    )


MESH = pl.DeviceIdType.MESH


def greet(partners):
    barrier = pltpu.get_barrier_semaphore()
    for partner in partners:
        pl.semaphore_signal(barrier, inc=1, device_id=partner, device_id_type=MESH)
    pl.semaphore_wait(barrier, len(partners))


def remote(src, dst, send, recv, partner):
    return pltpu.make_async_remote_copy(
        src_ref=src,
        dst_ref=dst,
        send_sem=send,
        recv_sem=recv,
        device_id=partner,
        device_id_type=MESH,
    )


def mlp_kernel(
    zs,
    ss,
    width,
    mid_ref,
    norm_ref,
    wg_hbm,
    wu_hbm,
    wd_hbm,
    out_ref,
    wg,
    wu,
    wd,
    cut,
    square,
    got,
    got_sq,
    normed,
    own_g,
    own_u,
    send_r,
    recv_r,
    send_l,
    recv_l,
    hid,
    down,
    parts,
    landed,
    sums,
    back,
    w_sem,
    a_send,
    a_recv,
    b_send,
    b_recv,
    rs_send,
    rs_recv,
    ag_send,
    ag_recv,
    d_send,
    d_recv,
    e_send,
    e_recv,
):
    z = lax.axis_index("req")
    s = lax.axis_index("seq")
    f32 = jnp.float32
    rows = mid_ref.shape[0]
    pieces = mid_ref.shape[1] // zs
    units = wg.shape[1]
    half = zs * rows // 2
    loads = [
        pltpu.make_async_copy(wg_hbm, wg, w_sem.at[0]),
        pltpu.make_async_copy(wu_hbm, wu, w_sem.at[1]),
        pltpu.make_async_copy(wd_hbm, wd, w_sem.at[2]),
    ]
    for load in loads:
        load.start()
    z_partners = [{"req": lax.rem(z + k, zs), "seq": s} for k in range(1, zs)]
    s_partners = [{"req": z, "seq": lax.rem(s + k, ss)} for k in range(1, ss)]

    total = jnp.zeros((8, rows), f32)
    for block in range(zs):
        piece = mid_ref[:, block * pieces : (block + 1) * pieces]
        cut[block] = piece
        value = piece.astype(f32)
        total += lax.dot_general(
            jnp.ones((8, pieces), f32),
            value * value,
            (((1,), (1,)), ((), ())),
            precision=lax.Precision.HIGHEST,
            preferred_element_type=f32,
        )
    square[...] = jnp.zeros_like(square)
    square[:, :rows] = total
    greet(z_partners + s_partners)
    first = []
    for k in range(1, zs):
        to = lax.rem(z + k, zs)
        first.append(
            remote(cut.at[to], got.at[s, z], a_send.at[0, k], a_recv.at[0, k], z_partners[k - 1])
        )
        first.append(
            remote(square, got_sq.at[s, z], a_send.at[1, k], a_recv.at[1, k], z_partners[k - 1])
        )
    for copy in first:
        copy.start()
    got[s, z] = cut[z]
    got_sq[s, z] = square[...]
    for copy in first:
        copy.wait_recv()
    second = []
    for k in range(1, ss):
        second.append(
            remote(got.at[s], got.at[s], b_send.at[0, k], b_recv.at[0, k], s_partners[k - 1])
        )
        second.append(
            remote(got_sq.at[s], got_sq.at[s], b_send.at[1, k], b_recv.at[1, k], s_partners[k - 1])
        )
    for copy in second:
        copy.start()
    for copy in second:
        copy.wait_recv()
    for group in range(zs):
        line = got_sq[0, group]
        for other in range(1, ss):
            line = line + got_sq[other, group]
        spread = lax.dot_general(
            line[:, :rows],
            jnp.full((8, 128), 0.125, f32),
            (((0,), (0,)), ((), ())),
            precision=lax.Precision.HIGHEST,
            preferred_element_type=f32,
        )
        inverse = lax.rsqrt(spread / D + EPSILON)[:, :1]
        for other in range(ss):
            gain = norm_ref[:, other * pieces : (other + 1) * pieces]
            normed[group * rows : (group + 1) * rows, other * pieces : (other + 1) * pieces] = (
                got[other, group].astype(f32) * inverse * gain
            ).astype(jnp.bfloat16)

    starts = list(range(0, units, width))
    count = len(starts)
    sizes = [min(width, units - start) for start in starts]
    padded = [-(-size // 128) * 128 for size in sizes]
    if sizes[-1] != padded[-1]:
        send_r[count - 1] = jnp.zeros_like(send_r[count - 1])
        send_l[count - 1] = jnp.zeros_like(send_l[count - 1])
        hid[count - 1] = jnp.zeros_like(hid[count - 1])
    down[...] = jnp.zeros_like(down)
    loads[0].wait()
    loads[1].wait()

    right = {"req": lax.rem(z + 1, zs), "seq": s}
    left = {"req": lax.rem(z + zs - 1, zs), "seq": s}

    def reduce_copy(way, p):
        src, dst, to = ((send_r, recv_r, right), (send_l, recv_l, left))[way]
        lanes = pl.ds(0, 2 * padded[p])
        return remote(
            src.at[p, :, lanes], dst.at[p, :, lanes], rs_send.at[way, p], rs_recv.at[way, p], to
        )

    def hidden_copy(way, p):
        place = (p, pl.ds(half * (1 - way), half), pl.ds(0, padded[p]))
        return remote(
            hid.at[place],
            hid.at[place],
            ag_send.at[way, p],
            ag_recv.at[way, p],
            (left, right)[way],
        )

    def reduce_step(way, p, place):
        size, pad = sizes[p], padded[p]
        base = half * (1 - way)
        cols = slice(starts[p], starts[p] + size)
        gate = own_g[base : base + half, cols]
        up = own_u[base : base + half, cols]
        if place > 0:
            reduce_copy(way, p).wait_recv()
            came = (recv_r, recv_l)[way]
            gate = gate + came[p, :, :size].astype(f32)
            up = up + came[p, :, pad : pad + size].astype(f32)
        if place < zs - 1:
            goes = (send_r, send_l)[way]
            goes[p, :, :size] = gate.astype(jnp.bfloat16)
            goes[p, :, pad : pad + size] = up.astype(jnp.bfloat16)
            reduce_copy(way, p).start()
        else:
            gate = gate.astype(jnp.bfloat16).astype(f32)
            up = up.astype(jnp.bfloat16).astype(f32)
            hid[p, base : base + half, :size] = (gate / (1.0 + jnp.exp(-gate)) * up).astype(
                jnp.bfloat16
            )
            hidden_copy(way, p).start()

    def down_step(p):
        down[...] += jnp.dot(
            hid[p, :, : sizes[p]],
            wd[starts[p] : starts[p] + sizes[p], :],
            preferred_element_type=f32,
        )

    lag = [0, 1, 3, 5, 7, 9, 11, 13, 15, 17]
    last = lag[2 * zs - 2]
    for i in range(count + last):
        if i < count:
            cols = slice(starts[i], starts[i] + sizes[i])
            own_g[:, cols] = jnp.dot(normed[...], wg[:, cols], preferred_element_type=f32)
            own_u[:, cols] = jnp.dot(normed[...], wu[:, cols], preferred_element_type=f32)
        for zz in range(zs):

            @pl.when(z == zz)
            def _(zz=zz, i=i):
                order = (0, 1) if zz < zs // 2 else (1, 0)
                for way in order:
                    place = zz if way == 0 else zs - 1 - zz
                    p = i - lag[place]
                    if 0 <= p < count:
                        reduce_step(way, p, place)
                for way in order[::-1]:
                    place = zs - 1 - zz if way == 0 else zz
                    p = i - lag[zs - 1 + place]
                    if place > 0 and 0 <= p < count:
                        hidden_copy(way, p).wait_recv()
                        if place < zs - 1:
                            hidden_copy(way, p).start()

        if i == last:
            loads[2].wait()
        if i >= last:
            down_step(i - last)

    for other in range(ss):
        parts[other] = down[:, other * pieces : (other + 1) * pieces].astype(jnp.bfloat16)
    third = []
    for k in range(1, ss):
        to = lax.rem(s + k, ss)
        third.append(
            remote(parts.at[to], landed.at[s], d_send.at[k], d_recv.at[k], s_partners[k - 1])
        )
    for copy in third:
        copy.start()
    landed[s] = parts[s]
    for copy in third:
        copy.wait_recv()
    whole = landed[0].astype(f32)
    for other in range(1, ss):
        whole = whole + landed[other].astype(f32)
    for group in range(zs):
        sums[group] = whole[group * rows : (group + 1) * rows]
    fourth = []
    for k in range(1, zs):
        to = lax.rem(z + k, zs)
        fourth.append(
            remote(sums.at[to], back.at[z], e_send.at[k], e_recv.at[k], z_partners[k - 1])
        )
    for copy in fourth:
        copy.start()
    back[z] = sums[z]
    for copy in fourth:
        copy.wait_recv()
    for block in range(zs):
        cols = slice(block * pieces, (block + 1) * pieces)
        out_ref[:, cols] = (mid_ref[:, cols].astype(f32) + back[block]).astype(jnp.bfloat16)

    for copy in first + second + third + fourth:
        copy.wait_send()
    for way in range(2):
        for p in range(count):

            @pl.when(z != (zs - 1 if way == 0 else 0))
            def _(way=way, p=p):
                reduce_copy(way, p).wait_send()

            @pl.when(z != (0 if way == 0 else zs - 1))
            def _(way=way, p=p):
                hidden_copy(way, p).wait_send()


def mlp(middle, norm, w_gate, w_up, w_down, zs, ss):
    rows, features = middle.shape
    pieces = features // zs
    depth, units = w_gate.shape
    quarter = w_down.shape[1]
    width = 512
    count = -(-units // width)
    everyone = zs * rows
    half = everyone // 2
    bf16, f32 = jnp.bfloat16, jnp.float32
    vmem = pl.BlockSpec(memory_space=pltpu.VMEM)
    hbm = pl.BlockSpec(memory_space=pl.ANY)
    dma = pltpu.SemaphoreType.DMA
    return pl.pallas_call(
        functools.partial(mlp_kernel, zs, ss, width),
        name="mlp",
        out_shape=jax.ShapeDtypeStruct(middle.shape, bf16),
        in_specs=[vmem, vmem, hbm, hbm, hbm],
        out_specs=vmem,
        scratch_shapes=[
            pltpu.VMEM(w_gate.shape, bf16),
            pltpu.VMEM(w_up.shape, bf16),
            pltpu.VMEM(w_down.shape, bf16),
            pltpu.VMEM((zs, rows, pieces), bf16),
            pltpu.VMEM((8, 128), f32),
            pltpu.VMEM((ss, zs, rows, pieces), bf16),
            pltpu.VMEM((ss, zs, 8, 128), f32),
            pltpu.VMEM((everyone, depth), bf16),
            pltpu.VMEM((everyone, units), f32),
            pltpu.VMEM((everyone, units), f32),
            pltpu.VMEM((count, half, 2 * width), bf16),
            pltpu.VMEM((count, half, 2 * width), bf16),
            pltpu.VMEM((count, half, 2 * width), bf16),
            pltpu.VMEM((count, half, 2 * width), bf16),
            pltpu.VMEM((count, everyone, width), bf16),
            pltpu.VMEM((everyone, quarter), f32),
            pltpu.VMEM((ss, everyone, pieces), bf16),
            pltpu.VMEM((ss, everyone, pieces), bf16),
            pltpu.VMEM((zs, rows, pieces), f32),
            pltpu.VMEM((zs, rows, pieces), f32),
            dma((3,)),
            dma((2, zs)),
            dma((2, zs)),
            dma((2, ss)),
            dma((2, ss)),
            dma((2, count)),
            dma((2, count)),
            dma((2, count)),
            dma((2, count)),
            dma((ss,)),
            dma((ss,)),
            dma((zs,)),
            dma((zs,)),
        ],
        compiler_params=pltpu.CompilerParams(
            collective_id=0, has_side_effects=True, vmem_limit_bytes=63 * 2**20
        ),
    )(middle, norm, w_gate, w_up, w_down)


def on_device(
    hidden_in,
    cache_lens,
    page_table,
    key_cache,
    value_cache,
    norm_attn,
    w_qkv,
    b_qkv,
    w_out,
    norm_mlp,
    w_gate,
    w_up,
    w_down,
):
    steps, requests, blocks, pieces = hidden_in.shape
    rows = steps * requests
    slots, per_page, _ = key_cache.shape
    group = H // KV
    quarter = D // blocks
    seq = quarter // pieces
    scale = 1.0 / math.sqrt(HD)
    slot_ids = lax.axis_index("seq") * slots + jnp.arange(slots, dtype=jnp.int32)
    matches = page_table[:, :, None] == slot_ids[None, None, :]
    live = jnp.any(matches, axis=(0, 1))
    owner = jnp.sum(
        jnp.where(matches, jnp.arange(requests, dtype=jnp.int32)[:, None, None], 0), axis=(0, 1)
    )
    logical = jnp.sum(
        jnp.where(matches, jnp.arange(page_table.shape[1], dtype=jnp.int32)[None, :, None], 0),
        axis=(0, 1),
    )
    owned = jnp.logical_and(
        jnp.arange(requests, dtype=jnp.int32)[None, :] == owner[:, None], live[:, None]
    )
    slot_length = jnp.sum(jnp.where(owned, cache_lens[None, :], 0), axis=1)
    positions = logical[:, None] * per_page + jnp.arange(per_page, dtype=jnp.int32)[None, :]

    flat = (
        lax.all_gather(hidden_in, "seq", axis=3, tiled=True).reshape(rows, D).astype(jnp.float32)
    )
    normed = (
        flat * lax.rsqrt(jnp.mean(flat * flat, axis=1, keepdims=True) + EPSILON) * norm_attn
    ).astype(jnp.bfloat16)
    columns = (
        jnp.dot(normed, w_qkv, preferred_element_type=jnp.float32) + b_qkv.astype(jnp.float32)
    ).astype(jnp.bfloat16)
    projected = lax.all_gather(columns, "seq", axis=1, tiled=True)
    position = (
        jnp.arange(steps, dtype=jnp.int32)[:, None] + cache_lens[None, :]
    ).reshape(rows)
    rotated = rotate(
        projected[:, : (H + KV) * HD].reshape(rows, H + KV, HD).astype(jnp.float32), position
    ).astype(jnp.bfloat16)
    queries = rotated[:, :H].reshape(steps, requests, KV, group, HD)
    new_keys = rotated[:, H:].reshape(steps, requests, KV * HD)
    new_values = projected[:, (H + KV) * HD :].reshape(steps, requests, KV * HD)
    slot_keys = jnp.take(new_keys, owner, axis=1)
    slot_values = jnp.take(new_values, owner, axis=1)
    for step in range(steps):
        write_here = jnp.logical_and(live[:, None], positions == (slot_length + step)[:, None])[
            :, :, None
        ]
        key_cache = jnp.where(write_here, slot_keys[step][:, None, :], key_cache)
        value_cache = jnp.where(write_here, slot_values[step][:, None, :], value_cache)

    slot_queries = jnp.take(queries, owner, axis=1)
    keys_view = key_cache.reshape(slots, per_page, KV, HD)
    values_view = value_cache.reshape(slots, per_page, KV, HD)
    scores = (
        jnp.einsum("tjkgd,jpkd->jktgp", slot_queries, keys_view, preferred_element_type=jnp.float32)
        * scale
    )
    last = slot_length[:, None] + jnp.arange(steps, dtype=jnp.int32)[None, :]
    valid = jnp.logical_and(
        live[:, None, None], positions[:, None, :] <= last[:, :, None]
    )[:, None, :, None, :]
    masked = jnp.where(valid, scores, NEGATIVE)
    page_max = jnp.max(masked, axis=4)
    weights = jnp.where(valid, jnp.exp(masked - page_max[..., None]), 0.0).astype(jnp.bfloat16)
    page_sum = jnp.sum(weights.astype(jnp.float32), axis=4)
    page_acc = jnp.einsum(
        "jktgp,jpkd->jktgd", weights, values_view, preferred_element_type=jnp.float32
    )
    spread = owned[:, :, None, None, None]
    candidates = jnp.where(spread, page_max[:, None], NEGATIVE)
    top = jnp.max(candidates, axis=0)
    factor = jnp.where(spread, jnp.exp(candidates - top[None]), 0.0)
    total = jnp.sum(factor * page_sum[:, None], axis=0)
    summed = jnp.sum(factor[..., None] * page_acc[:, None], axis=0)
    def by_head(value):
        value = jnp.moveaxis(value, 0, 3)
        value = jnp.swapaxes(value, 1, 2)
        return value.reshape((seq, H // seq, rows) + value.shape[4:])

    packed = jnp.concatenate(
        [
            by_head(summed).reshape(seq, -1),
            by_head(top).reshape(seq, -1),
            by_head(total).reshape(seq, -1),
        ],
        axis=1,
    )
    packed = lax.all_to_all(packed, "seq", split_axis=0, concat_axis=0, tiled=True)
    count = (H // seq) * rows
    part_acc = packed[:, : count * HD].reshape(seq, count, HD)
    part_top = packed[:, count * HD : count * (HD + 1)]
    part_sum = packed[:, count * (HD + 1) :]
    best = jnp.max(part_top, axis=0)
    share = jnp.exp(part_top - best[None])
    denominator = jnp.sum(share * part_sum, axis=0)
    numerator = jnp.sum(share[..., None] * part_acc, axis=0)
    heads = (numerator / denominator[:, None]).astype(jnp.bfloat16)
    heads = jnp.swapaxes(heads.reshape(H // seq, rows, HD), 0, 1).reshape(rows, -1)
    attended = lax.all_gather(heads, "seq", axis=1, tiled=True)
    branch_out = jnp.dot(
        attended, w_out.reshape(H * HD, blocks * pieces), preferred_element_type=jnp.float32
    ).reshape(rows, blocks, pieces)
    current = hidden_in.reshape(rows, blocks, pieces).astype(jnp.float32)
    middle = (current + branch_out).astype(jnp.bfloat16)
    zs = D // w_gate.shape[0]
    if pieces % 128 == 0 and zs == blocks and zs % 2 == 0 and rows <= 128 and rows % 16 == 0:
        gain = lax.dynamic_slice(norm_mlp, (lax.axis_index("req") * quarter,), (quarter,))
        output = mlp(
            middle.reshape(rows, blocks * pieces),
            gain.reshape(1, quarter),
            w_gate,
            w_up,
            w_down,
            zs,
            seq,
        )
        return (output.reshape(hidden_in.shape), key_cache, value_cache)
    rows_mid = lax.all_gather(middle, "seq", axis=2, tiled=True).astype(jnp.float32)
    inverse = lax.rsqrt(jnp.mean(rows_mid * rows_mid, axis=(1, 2), keepdims=True) + EPSILON)
    normed_mid = (rows_mid * inverse * norm_mlp.reshape(blocks, quarter)).astype(jnp.bfloat16)
    mine = lax.all_to_all(normed_mid, "req", split_axis=1, concat_axis=0, tiled=True).reshape(
        -1, quarter
    )
    gate_part = jnp.dot(mine, w_gate, preferred_element_type=jnp.float32).astype(jnp.bfloat16)
    up_part = jnp.dot(mine, w_up, preferred_element_type=jnp.float32).astype(jnp.bfloat16)
    gate_sum = lax.psum_scatter(gate_part, "req", scatter_dimension=0, tiled=True)
    up_sum = lax.psum_scatter(up_part, "req", scatter_dimension=0, tiled=True)
    hidden_part = (
        jax.nn.silu(gate_sum.astype(jnp.float32)) * up_sum.astype(jnp.float32)
    ).astype(jnp.bfloat16)
    hidden = lax.all_gather(hidden_part, "req", axis=0, tiled=True)
    down = jnp.dot(hidden, w_down, preferred_element_type=jnp.float32)
    sums = lax.psum_scatter(
        down.reshape(down.shape[0], 1, quarter).astype(jnp.bfloat16),
        "seq",
        scatter_dimension=2,
        tiled=True,
    ).astype(jnp.float32)
    back = lax.all_to_all(sums, "req", split_axis=0, concat_axis=1, tiled=True)
    output = (middle.astype(jnp.float32) + back).astype(jnp.bfloat16)
    return (output.reshape(hidden_in.shape), key_cache, value_cache)


def solution(mesh):
    in_specs = (
        P(None, "req", None, "seq"),
        P("req"),
        P("req", None),
        P(("req", "seq"), None, None),
        P(("req", "seq"), None, None),
        P(),
        P(None, "seq"),
        P("seq"),
        P(None, None, "seq"),
        P(),
        P("req", "seq"),
        P("req", "seq"),
        P("seq", "req"),
    )
    out_specs = (
        P(None, "req", None, "seq"),
        P(("req", "seq"), None, None),
        P(("req", "seq"), None, None),
    )
    return jax.shard_map(
        on_device, mesh=mesh, in_specs=in_specs, out_specs=out_specs, check_vma=False
    )
```

```python
import functools
import math

import jax
import jax.numpy as jnp
from jax import lax
from jax.experimental import pallas as pl
from jax.experimental.pallas import tpu as pltpu
from jax.sharding import PartitionSpec as P

D = 8192
H = 64
KV = 8
HD = 128
STEPS = 4


EPSILON = 1e-06
THETA = 1000000.0
NEGATIVE = -1e30


def rotate(heads, position):
    half = heads.shape[-1] // 2
    freq = THETA ** (-(jnp.arange(half, dtype=jnp.float32) * 2.0 / heads.shape[-1]))
    angle = position.astype(jnp.float32)[:, None, None] * freq[None, None, :]
    cosine = jnp.cos(angle)
    sine = jnp.sin(angle)
    first = heads[..., :half]
    second = heads[..., half:]
    return jnp.concatenate(
        [first * cosine - second * sine, second * cosine + first * sine], axis=-1
    )


MESH = pl.DeviceIdType.MESH


def greet(partners):
    barrier = pltpu.get_barrier_semaphore()
    for partner in partners:
        pl.semaphore_signal(barrier, inc=1, device_id=partner, device_id_type=MESH)
    pl.semaphore_wait(barrier, len(partners))


def remote(src, dst, send, recv, partner):
    return pltpu.make_async_remote_copy(
        src_ref=src,
        dst_ref=dst,
        send_sem=send,
        recv_sem=recv,
        device_id=partner,
        device_id_type=MESH,
    )


def mlp_kernel(
    zs,
    ss,
    width,
    mid_ref,
    norm_ref,
    wg_hbm,
    wu_hbm,
    wd_hbm,
    out_ref,
    wg,
    wu,
    wd,
    cut,
    square,
    got,
    got_sq,
    normed,
    own_g,
    own_u,
    send_r,
    recv_r,
    send_l,
    recv_l,
    hid,
    down,
    parts,
    landed,
    sums,
    back,
    w_sem,
    a_send,
    a_recv,
    b_send,
    b_recv,
    rs_send,
    rs_recv,
    ag_send,
    ag_recv,
    d_send,
    d_recv,
    e_send,
    e_recv,
):
    z = lax.axis_index("req")
    s = lax.axis_index("seq")
    f32 = jnp.float32
    rows = mid_ref.shape[0]
    pieces = mid_ref.shape[1] // zs
    units = wg.shape[0]
    half = zs * rows // 2
    loads = [
        pltpu.make_async_copy(wg_hbm, wg, w_sem.at[0]),
        pltpu.make_async_copy(wu_hbm, wu, w_sem.at[1]),
        pltpu.make_async_copy(wd_hbm, wd, w_sem.at[2]),
    ]
    for load in loads:
        load.start()
    z_partners = [{"req": lax.rem(z + k, zs), "seq": s} for k in range(1, zs)]
    s_partners = [{"req": z, "seq": lax.rem(s + k, ss)} for k in range(1, ss)]

    total = jnp.zeros((8, rows), f32)
    for block in range(zs):
        piece = mid_ref[:, block * pieces : (block + 1) * pieces]
        cut[block] = piece
        value = piece.astype(f32)
        total += lax.dot_general(
            jnp.ones((8, pieces), f32),
            value * value,
            (((1,), (1,)), ((), ())),
            precision=lax.Precision.HIGHEST,
            preferred_element_type=f32,
        )
    square[...] = jnp.zeros_like(square)
    square[:, :rows] = total
    greet(z_partners + s_partners)
    first = []
    for k in range(1, zs):
        to = lax.rem(z + k, zs)
        first.append(
            remote(cut.at[to], got.at[s, z], a_send.at[0, k], a_recv.at[0, k], z_partners[k - 1])
        )
        first.append(
            remote(square, got_sq.at[s, z], a_send.at[1, k], a_recv.at[1, k], z_partners[k - 1])
        )
    for copy in first:
        copy.start()
    got[s, z] = cut[z]
    got_sq[s, z] = square[...]
    for copy in first:
        copy.wait_recv()
    second = []
    for k in range(1, ss):
        second.append(
            remote(got.at[s], got.at[s], b_send.at[0, k], b_recv.at[0, k], s_partners[k - 1])
        )
        second.append(
            remote(got_sq.at[s], got_sq.at[s], b_send.at[1, k], b_recv.at[1, k], s_partners[k - 1])
        )
    for copy in second:
        copy.start()
    for copy in second:
        copy.wait_recv()
    for group in range(zs):
        line = got_sq[0, group]
        for other in range(1, ss):
            line = line + got_sq[other, group]
        spread = lax.dot_general(
            line[:, :rows],
            jnp.full((8, 128), 0.125, f32),
            (((0,), (0,)), ((), ())),
            precision=lax.Precision.HIGHEST,
            preferred_element_type=f32,
        )
        inverse = lax.rsqrt(spread / D + EPSILON)[:, :1]
        for other in range(ss):
            gain = norm_ref[:, other * pieces : (other + 1) * pieces]
            normed[group * rows : (group + 1) * rows, other * pieces : (other + 1) * pieces] = (
                got[other, group].astype(f32) * inverse * gain
            ).astype(jnp.bfloat16)

    starts = list(range(0, units, width))
    count = len(starts)
    sizes = [min(width, units - start) for start in starts]
    padded = [-(-size // 128) * 128 for size in sizes]
    if sizes[-1] != padded[-1]:
        send_r[count - 1] = jnp.zeros_like(send_r[count - 1])
        send_l[count - 1] = jnp.zeros_like(send_l[count - 1])
        hid[count - 1] = jnp.zeros_like(hid[count - 1])
    down[...] = jnp.zeros_like(down)
    loads[0].wait()
    loads[1].wait()

    right = {"req": lax.rem(z + 1, zs), "seq": s}
    left = {"req": lax.rem(z + zs - 1, zs), "seq": s}

    def reduce_copy(way, p):
        src, dst, to = ((send_r, recv_r, right), (send_l, recv_l, left))[way]
        lanes = pl.ds(0, 2 * padded[p])
        return remote(
            src.at[p, :, lanes], dst.at[p, :, lanes], rs_send.at[way, p], rs_recv.at[way, p], to
        )

    def hidden_copy(way, p):
        place = (p, pl.ds(half * (1 - way), half), pl.ds(0, padded[p]))
        return remote(
            hid.at[place],
            hid.at[place],
            ag_send.at[way, p],
            ag_recv.at[way, p],
            (left, right)[way],
        )

    def reduce_step(way, p, place):
        size, pad = sizes[p], padded[p]
        base = half * (1 - way)
        cols = slice(starts[p], starts[p] + size)
        gate = own_g[base : base + half, cols]
        up = own_u[base : base + half, cols]
        if place > 0:
            reduce_copy(way, p).wait_recv()
            came = (recv_r, recv_l)[way]
            gate = gate + came[p, :, :size].astype(f32)
            up = up + came[p, :, pad : pad + size].astype(f32)
        if place < zs - 1:
            goes = (send_r, send_l)[way]
            goes[p, :, :size] = gate.astype(jnp.bfloat16)
            goes[p, :, pad : pad + size] = up.astype(jnp.bfloat16)
            reduce_copy(way, p).start()
        else:
            gate = gate.astype(jnp.bfloat16).astype(f32)
            up = up.astype(jnp.bfloat16).astype(f32)
            hid[p, base : base + half, :size] = (gate / (1.0 + jnp.exp(-gate)) * up).astype(
                jnp.bfloat16
            )
            hidden_copy(way, p).start()

    def down_step(p):
        down[...] += jnp.dot(
            hid[p, :, : sizes[p]],
            wd[starts[p] : starts[p] + sizes[p], :],
            preferred_element_type=f32,
        )

    nt = (((1,), (1,)), ((), ()))
    lag = [0, 1, 3, 5, 7, 9, 11, 13, 15, 17]
    last = lag[2 * zs - 2]
    for i in range(count + last):
        if i < count:
            cols = slice(starts[i], starts[i] + sizes[i])
            own_g[:, cols] = lax.dot_general(normed[...], wg[cols, :], nt, preferred_element_type=f32)
            own_u[:, cols] = lax.dot_general(normed[...], wu[cols, :], nt, preferred_element_type=f32)
        for zz in range(zs):

            @pl.when(z == zz)
            def _(zz=zz, i=i):
                order = (0, 1) if zz < zs // 2 else (1, 0)
                for way in order:
                    place = zz if way == 0 else zs - 1 - zz
                    p = i - lag[place]
                    if 0 <= p < count:
                        reduce_step(way, p, place)
                for way in order[::-1]:
                    place = zs - 1 - zz if way == 0 else zz
                    p = i - lag[zs - 1 + place]
                    if place > 0 and 0 <= p < count:
                        hidden_copy(way, p).wait_recv()
                        if place < zs - 1:
                            hidden_copy(way, p).start()

        if i == last:
            loads[2].wait()
        if i >= last:
            down_step(i - last)

    for other in range(ss):
        parts[other] = down[:, other * pieces : (other + 1) * pieces].astype(jnp.bfloat16)
    third = []
    for k in range(1, ss):
        to = lax.rem(s + k, ss)
        third.append(
            remote(parts.at[to], landed.at[s], d_send.at[k], d_recv.at[k], s_partners[k - 1])
        )
    for copy in third:
        copy.start()
    landed[s] = parts[s]
    for copy in third:
        copy.wait_recv()
    whole = landed[0].astype(f32)
    for other in range(1, ss):
        whole = whole + landed[other].astype(f32)
    for group in range(zs):
        sums[group] = whole[group * rows : (group + 1) * rows]
    fourth = []
    for k in range(1, zs):
        to = lax.rem(z + k, zs)
        fourth.append(
            remote(sums.at[to], back.at[z], e_send.at[k], e_recv.at[k], z_partners[k - 1])
        )
    for copy in fourth:
        copy.start()
    back[z] = sums[z]
    for copy in fourth:
        copy.wait_recv()
    for block in range(zs):
        cols = slice(block * pieces, (block + 1) * pieces)
        out_ref[:, cols] = (mid_ref[:, cols].astype(f32) + back[block]).astype(jnp.bfloat16)

    for copy in first + second + third + fourth:
        copy.wait_send()
    for way in range(2):
        for p in range(count):

            @pl.when(z != (zs - 1 if way == 0 else 0))
            def _(way=way, p=p):
                reduce_copy(way, p).wait_send()

            @pl.when(z != (0 if way == 0 else zs - 1))
            def _(way=way, p=p):
                hidden_copy(way, p).wait_send()


def mlp(middle, norm, w_gate, w_up, w_down, zs, ss):
    rows, features = middle.shape
    pieces = features // zs
    units, depth = w_gate.shape
    quarter = w_down.shape[1]
    width = 512
    count = -(-units // width)
    everyone = zs * rows
    half = everyone // 2
    bf16, f32 = jnp.bfloat16, jnp.float32
    vmem = pl.BlockSpec(memory_space=pltpu.VMEM)
    hbm = pl.BlockSpec(memory_space=pl.ANY)
    dma = pltpu.SemaphoreType.DMA
    return pl.pallas_call(
        functools.partial(mlp_kernel, zs, ss, width),
        name="mlp",
        out_shape=jax.ShapeDtypeStruct(middle.shape, bf16),
        in_specs=[vmem, vmem, hbm, hbm, hbm],
        out_specs=vmem,
        scratch_shapes=[
            pltpu.VMEM(w_gate.shape, bf16),
            pltpu.VMEM(w_up.shape, bf16),
            pltpu.VMEM(w_down.shape, bf16),
            pltpu.VMEM((zs, rows, pieces), bf16),
            pltpu.VMEM((8, 128), f32),
            pltpu.VMEM((ss, zs, rows, pieces), bf16),
            pltpu.VMEM((ss, zs, 8, 128), f32),
            pltpu.VMEM((everyone, depth), bf16),
            pltpu.VMEM((everyone, units), f32),
            pltpu.VMEM((everyone, units), f32),
            pltpu.VMEM((count, half, 2 * width), bf16),
            pltpu.VMEM((count, half, 2 * width), bf16),
            pltpu.VMEM((count, half, 2 * width), bf16),
            pltpu.VMEM((count, half, 2 * width), bf16),
            pltpu.VMEM((count, everyone, width), bf16),
            pltpu.VMEM((everyone, quarter), f32),
            pltpu.VMEM((ss, everyone, pieces), bf16),
            pltpu.VMEM((ss, everyone, pieces), bf16),
            pltpu.VMEM((zs, rows, pieces), f32),
            pltpu.VMEM((zs, rows, pieces), f32),
            dma((3,)),
            dma((2, zs)),
            dma((2, zs)),
            dma((2, ss)),
            dma((2, ss)),
            dma((2, count)),
            dma((2, count)),
            dma((2, count)),
            dma((2, count)),
            dma((ss,)),
            dma((ss,)),
            dma((zs,)),
            dma((zs,)),
        ],
        compiler_params=pltpu.CompilerParams(
            collective_id=0, has_side_effects=True, vmem_limit_bytes=63 * 2**20
        ),
    )(middle, norm, w_gate, w_up, w_down)


def project_kernel(
    zs,
    ss,
    x_ref,
    norm_ref,
    bias_ref,
    w_hbm,
    out_ref,
    w,
    own,
    got,
    normed,
    sent,
    columns,
    w_sem,
    a_send,
    a_recv,
    b_send,
    b_recv,
):
    z = lax.axis_index("req")
    s = lax.axis_index("seq")
    f32 = jnp.float32
    rows, features = x_ref.shape
    blocks = norm_ref.shape[0]
    pieces = features // blocks
    mine = w.shape[1]
    parts = 4
    depth = D // parts
    loads = [
        pltpu.make_async_copy(
            w_hbm.at[pl.ds(part * depth, depth)], w.at[pl.ds(part * depth, depth)], w_sem.at[part]
        )
        for part in range(parts)
    ]
    for load in loads:
        load.start()
    partners = [{"req": z, "seq": lax.rem(s + k, ss)} for k in range(1, ss)]
    own[...] = x_ref[...]
    greet(partners)
    first = [
        remote(own, got.at[s], a_send.at[k], a_recv.at[k], partners[k - 1]) for k in range(1, ss)
    ]
    for copy in first:
        copy.start()
    got[s] = own[...]
    for copy in first:
        copy.wait_recv()
    total = jnp.zeros((rows, 1), f32)
    for other in range(ss):
        value = got[other].astype(f32)
        total += jnp.sum(value * value, axis=1, keepdims=True)
    inverse = lax.rsqrt(total / D + EPSILON)
    for other in range(ss):
        for block in range(blocks):
            lanes = slice(other * pieces, (other + 1) * pieces)
            base = block * ss * pieces + other * pieces
            value = got[other, :, block * pieces : (block + 1) * pieces].astype(f32)
            normed[:, base : base + pieces] = (
                value * inverse * norm_ref[block : block + 1, lanes]
            ).astype(jnp.bfloat16)
    result = jnp.zeros((rows, mine), f32)
    for part in range(parts):
        loads[part].wait()
        span = slice(part * depth, (part + 1) * depth)
        result += jnp.dot(normed[:, span], w[span, :], preferred_element_type=f32)
    sent[...] = (result + bias_ref[...].astype(f32)).astype(jnp.bfloat16)
    second = [
        remote(sent, columns.at[s], b_send.at[k], b_recv.at[k], partners[k - 1])
        for k in range(1, ss)
    ]
    for copy in second:
        copy.start()
    columns[s] = sent[...]
    for copy in second:
        copy.wait_recv()
    for other in range(ss):
        out_ref[:, other * mine : (other + 1) * mine] = columns[other]
    for copy in first + second:
        copy.wait_send()


def project(x, norm, bias, w, zs, ss):
    rows, features = x.shape
    mine = w.shape[1]
    bf16 = jnp.bfloat16
    vmem = pl.BlockSpec(memory_space=pltpu.VMEM)
    dma = pltpu.SemaphoreType.DMA
    return pl.pallas_call(
        functools.partial(project_kernel, zs, ss),
        name="project",
        out_shape=jax.ShapeDtypeStruct((rows, ss * mine), bf16),
        in_specs=[vmem, vmem, vmem, pl.BlockSpec(memory_space=pl.ANY)],
        out_specs=vmem,
        scratch_shapes=[
            pltpu.VMEM(w.shape, bf16),
            pltpu.VMEM((rows, features), bf16),
            pltpu.VMEM((ss, rows, features), bf16),
            pltpu.VMEM((rows, D), bf16),
            pltpu.VMEM((rows, mine), bf16),
            pltpu.VMEM((ss, rows, mine), bf16),
            dma((4,)),
            dma((ss,)),
            dma((ss,)),
            dma((ss,)),
            dma((ss,)),
        ],
        compiler_params=pltpu.CompilerParams(
            collective_id=1, has_side_effects=True, vmem_limit_bytes=48 * 2**20
        ),
    )(x, norm, bias, w)


def merge_kernel(
    zs,
    ss,
    acc_ref,
    stat_ref,
    x_ref,
    w_hbm,
    out_ref,
    w,
    acc,
    stat,
    got,
    got_stat,
    heads,
    everyone,
    joined,
    w_sem,
    a_send,
    a_recv,
    b_send,
    b_recv,
):
    z = lax.axis_index("req")
    s = lax.axis_index("seq")
    f32 = jnp.float32
    rows = x_ref.shape[0]
    per = H // ss
    parts = 4
    depth = D // parts
    loads = [
        pltpu.make_async_copy(
            w_hbm.at[pl.ds(part * depth, depth)], w.at[pl.ds(part * depth, depth)], w_sem.at[part]
        )
        for part in range(parts)
    ]
    for load in loads:
        load.start()
    partners = [{"req": z, "seq": lax.rem(s + k, ss)} for k in range(1, ss)]
    acc[...] = acc_ref[...]
    stat[...] = stat_ref[...]
    greet(partners)
    first = []
    for k in range(1, ss):
        to = lax.rem(s + k, ss)
        first.append(
            remote(stat.at[to], got_stat.at[s], a_send.at[1, k], a_recv.at[1, k], partners[k - 1])
        )
        first.append(
            remote(acc.at[to], got.at[s], a_send.at[0, k], a_recv.at[0, k], partners[k - 1])
        )
    for copy in first:
        copy.start()
    got[s] = acc[s]
    got_stat[s] = stat[s]
    for copy in first:
        copy.wait_recv()
    lines = per * rows // 128
    best = got_stat[0, :lines]
    for other in range(1, ss):
        best = jnp.maximum(best, got_stat[other, :lines])
    shares = [jnp.exp(got_stat[other, :lines] - best) for other in range(ss)]
    denominator = shares[0] * got_stat[0, lines : 2 * lines]
    for other in range(1, ss):
        denominator = denominator + shares[other] * got_stat[other, lines : 2 * lines]
    tall = jnp.transpose(
        jnp.concatenate([share / denominator for share in shares], axis=0)
    )
    for line in range(lines):
        span = slice(line * 128, (line + 1) * 128)
        value = got[0, span, :] * tall[:, line : line + 1]
        for other in range(1, ss):
            at = other * lines + line
            value = value + got[other, span, :] * tall[:, at : at + 1]
        heads[span, :] = value.astype(jnp.bfloat16)
    second = [
        remote(heads, everyone.at[s], b_send.at[k], b_recv.at[k], partners[k - 1])
        for k in range(1, ss)
    ]
    for copy in second:
        copy.start()
    everyone[s] = heads[...]
    for copy in second:
        copy.wait_recv()
    for other in range(ss):
        for head in range(per):
            base = (other * per + head) * HD
            joined[:, base : base + HD] = everyone[other, head * rows : (head + 1) * rows, :]
    result = x_ref[...].astype(f32)
    for part in range(parts):
        loads[part].wait()
        span = slice(part * depth, (part + 1) * depth)
        result += jnp.dot(joined[:, span], w[span, :], preferred_element_type=f32)
    out_ref[...] = result.astype(jnp.bfloat16)
    for copy in first + second:
        copy.wait_send()


def merge(acc, stat, x, w, zs, ss):
    rows, features = x.shape
    bf16, f32 = jnp.bfloat16, jnp.float32
    vmem = pl.BlockSpec(memory_space=pltpu.VMEM)
    dma = pltpu.SemaphoreType.DMA
    return pl.pallas_call(
        functools.partial(merge_kernel, zs, ss),
        name="merge",
        out_shape=jax.ShapeDtypeStruct((rows, features), bf16),
        in_specs=[vmem, vmem, vmem, pl.BlockSpec(memory_space=pl.ANY)],
        out_specs=vmem,
        scratch_shapes=[
            pltpu.VMEM(w.shape, bf16),
            pltpu.VMEM(acc.shape, f32),
            pltpu.VMEM(stat.shape, f32),
            pltpu.VMEM(acc.shape, f32),
            pltpu.VMEM(stat.shape, f32),
            pltpu.VMEM(acc.shape[1:], bf16),
            pltpu.VMEM(acc.shape, bf16),
            pltpu.VMEM((rows, H * HD), bf16),
            dma((4,)),
            dma((2, ss)),
            dma((2, ss)),
            dma((ss,)),
            dma((ss,)),
        ],
        compiler_params=pltpu.CompilerParams(
            collective_id=2, has_side_effects=True, vmem_limit_bytes=48 * 2**20
        ),
    )(acc, stat, x, w)


def on_device(
    hidden_in,
    cache_lens,
    page_table,
    key_cache,
    value_cache,
    norm_attn,
    w_qkv,
    b_qkv,
    w_out,
    norm_mlp,
    w_gate,
    w_up,
    w_down,
):
    steps, requests, blocks, pieces = hidden_in.shape
    rows = steps * requests
    slots, per_page, _ = key_cache.shape
    group = H // KV
    quarter = D // blocks
    seq = quarter // pieces
    scale = 1.0 / math.sqrt(HD)
    zs = D // w_gate.shape[0]
    fast = (
        pieces % 128 == 0
        and w_qkv.shape[1] % 128 == 0
        and zs == blocks
        and zs % 2 == 0
        and rows <= 128
        and rows % 16 == 0
        and H % seq == 0
        and (H // seq) * rows % 128 == 0
    )
    slot_ids = lax.axis_index("seq") * slots + jnp.arange(slots, dtype=jnp.int32)
    matches = page_table[:, :, None] == slot_ids[None, None, :]
    live = jnp.any(matches, axis=(0, 1))
    owner = jnp.sum(
        jnp.where(matches, jnp.arange(requests, dtype=jnp.int32)[:, None, None], 0), axis=(0, 1)
    )
    logical = jnp.sum(
        jnp.where(matches, jnp.arange(page_table.shape[1], dtype=jnp.int32)[None, :, None], 0),
        axis=(0, 1),
    )
    owned = jnp.logical_and(
        jnp.arange(requests, dtype=jnp.int32)[None, :] == owner[:, None], live[:, None]
    )
    slot_length = jnp.sum(jnp.where(owned, cache_lens[None, :], 0), axis=1)
    positions = logical[:, None] * per_page + jnp.arange(per_page, dtype=jnp.int32)[None, :]

    if fast:
        projected = project(
            hidden_in.reshape(rows, blocks * pieces),
            norm_attn.reshape(blocks, quarter),
            b_qkv.reshape(1, -1),
            w_qkv,
            zs,
            seq,
        )
    else:
        flat = (
            lax.all_gather(hidden_in, "seq", axis=3, tiled=True).reshape(rows, D).astype(jnp.float32)
        )
        normed = (
            flat * lax.rsqrt(jnp.mean(flat * flat, axis=1, keepdims=True) + EPSILON) * norm_attn
        ).astype(jnp.bfloat16)
        columns = (
            jnp.dot(normed, w_qkv, preferred_element_type=jnp.float32) + b_qkv.astype(jnp.float32)
        ).astype(jnp.bfloat16)
        projected = lax.all_gather(columns, "seq", axis=1, tiled=True)
    position = (
        jnp.arange(steps, dtype=jnp.int32)[:, None] + cache_lens[None, :]
    ).reshape(rows)
    rotated = rotate(
        projected[:, : (H + KV) * HD].reshape(rows, H + KV, HD).astype(jnp.float32), position
    ).astype(jnp.bfloat16)
    queries = rotated[:, :H].reshape(steps, requests, KV, group, HD)
    new_keys = rotated[:, H:].reshape(steps, requests, KV * HD)
    new_values = projected[:, (H + KV) * HD :].reshape(steps, requests, KV * HD)
    slot_keys = jnp.take(new_keys, owner, axis=1)
    slot_values = jnp.take(new_values, owner, axis=1)
    for step in range(steps):
        write_here = jnp.logical_and(live[:, None], positions == (slot_length + step)[:, None])[
            :, :, None
        ]
        key_cache = jnp.where(write_here, slot_keys[step][:, None, :], key_cache)
        value_cache = jnp.where(write_here, slot_values[step][:, None, :], value_cache)

    slot_queries = jnp.take(queries, owner, axis=1)
    keys_view = key_cache.reshape(slots, per_page, KV, HD)
    values_view = value_cache.reshape(slots, per_page, KV, HD)
    scores = (
        jnp.einsum("tjkgd,jpkd->jktgp", slot_queries, keys_view, preferred_element_type=jnp.float32)
        * scale
    )
    last = slot_length[:, None] + jnp.arange(steps, dtype=jnp.int32)[None, :]
    valid = jnp.logical_and(
        live[:, None, None], positions[:, None, :] <= last[:, :, None]
    )[:, None, :, None, :]
    masked = jnp.where(valid, scores, NEGATIVE)
    page_max = jnp.max(masked, axis=4)
    weights = jnp.where(valid, jnp.exp(masked - page_max[..., None]), 0.0).astype(jnp.bfloat16)
    page_sum = jnp.sum(weights.astype(jnp.float32), axis=4)
    page_acc = jnp.einsum(
        "jktgp,jpkd->jktgd", weights, values_view, preferred_element_type=jnp.float32
    )
    spread = owned[:, :, None, None, None]
    candidates = jnp.where(spread, page_max[:, None], NEGATIVE)
    top = jnp.max(candidates, axis=0)
    factor = jnp.where(spread, jnp.exp(candidates - top[None]), 0.0)
    total = jnp.sum(factor * page_sum[:, None], axis=0)
    summed = jnp.sum(factor[..., None] * page_acc[:, None], axis=0)
    def by_head(value):
        value = jnp.moveaxis(value, 0, 3)
        value = jnp.swapaxes(value, 1, 2)
        return value.reshape((seq, H // seq, rows) + value.shape[4:])

    if fast:
        stat = jnp.concatenate([by_head(top), by_head(total)], axis=1).reshape(seq, -1, 128)
        middle = merge(
            by_head(summed).reshape(seq, -1, HD),
            stat,
            hidden_in.reshape(rows, blocks * pieces),
            w_out.reshape(H * HD, blocks * pieces),
            zs,
            seq,
        )
    else:
        packed = jnp.concatenate(
            [
                by_head(summed).reshape(seq, -1),
                by_head(top).reshape(seq, -1),
                by_head(total).reshape(seq, -1),
            ],
            axis=1,
        )
        packed = lax.all_to_all(packed, "seq", split_axis=0, concat_axis=0, tiled=True)
        count = (H // seq) * rows
        part_acc = packed[:, : count * HD].reshape(seq, count, HD)
        part_top = packed[:, count * HD : count * (HD + 1)]
        part_sum = packed[:, count * (HD + 1) :]
        best = jnp.max(part_top, axis=0)
        share = jnp.exp(part_top - best[None])
        denominator = jnp.sum(share * part_sum, axis=0)
        numerator = jnp.sum(share[..., None] * part_acc, axis=0)
        heads = (numerator / denominator[:, None]).astype(jnp.bfloat16)
        heads = jnp.swapaxes(heads.reshape(H // seq, rows, HD), 0, 1).reshape(rows, -1)
        attended = lax.all_gather(heads, "seq", axis=1, tiled=True)
        branch_out = jnp.dot(
            attended, w_out.reshape(H * HD, blocks * pieces), preferred_element_type=jnp.float32
        ).reshape(rows, blocks, pieces)
        current = hidden_in.reshape(rows, blocks, pieces).astype(jnp.float32)
        middle = (current + branch_out).astype(jnp.bfloat16)
    if fast:
        gain = lax.dynamic_slice(norm_mlp, (lax.axis_index("req") * quarter,), (quarter,))
        output = mlp(
            middle.reshape(rows, blocks * pieces),
            gain.reshape(1, quarter),
            jnp.swapaxes(w_gate, 0, 1),
            jnp.swapaxes(w_up, 0, 1),
            w_down,
            zs,
            seq,
        )
        return (output.reshape(hidden_in.shape), key_cache, value_cache)
    rows_mid = lax.all_gather(middle, "seq", axis=2, tiled=True).astype(jnp.float32)
    inverse = lax.rsqrt(jnp.mean(rows_mid * rows_mid, axis=(1, 2), keepdims=True) + EPSILON)
    normed_mid = (rows_mid * inverse * norm_mlp.reshape(blocks, quarter)).astype(jnp.bfloat16)
    mine = lax.all_to_all(normed_mid, "req", split_axis=1, concat_axis=0, tiled=True).reshape(
        -1, quarter
    )
    gate_part = jnp.dot(mine, w_gate, preferred_element_type=jnp.float32).astype(jnp.bfloat16)
    up_part = jnp.dot(mine, w_up, preferred_element_type=jnp.float32).astype(jnp.bfloat16)
    gate_sum = lax.psum_scatter(gate_part, "req", scatter_dimension=0, tiled=True)
    up_sum = lax.psum_scatter(up_part, "req", scatter_dimension=0, tiled=True)
    hidden_part = (
        jax.nn.silu(gate_sum.astype(jnp.float32)) * up_sum.astype(jnp.float32)
    ).astype(jnp.bfloat16)
    hidden = lax.all_gather(hidden_part, "req", axis=0, tiled=True)
    down = jnp.dot(hidden, w_down, preferred_element_type=jnp.float32)
    sums = lax.psum_scatter(
        down.reshape(down.shape[0], 1, quarter).astype(jnp.bfloat16),
        "seq",
        scatter_dimension=2,
        tiled=True,
    ).astype(jnp.float32)
    back = lax.all_to_all(sums, "req", split_axis=0, concat_axis=1, tiled=True)
    output = (middle.astype(jnp.float32) + back).astype(jnp.bfloat16)
    return (output.reshape(hidden_in.shape), key_cache, value_cache)


def solution(mesh):
    in_specs = (
        P(None, "req", None, "seq"),
        P("req"),
        P("req", None),
        P(("req", "seq"), None, None),
        P(("req", "seq"), None, None),
        P(),
        P(None, "seq"),
        P("seq"),
        P(None, None, "seq"),
        P(),
        P("req", "seq"),
        P("req", "seq"),
        P("seq", "req"),
    )
    out_specs = (
        P(None, "req", None, "seq"),
        P(("req", "seq"), None, None),
        P(("req", "seq"), None, None),
    )
    return jax.shard_map(
        on_device, mesh=mesh, in_specs=in_specs, out_specs=out_specs, check_vma=False
    )
```

```python
import functools
import math

import jax
import jax.numpy as jnp
from jax import lax
from jax.experimental import pallas as pl
from jax.experimental.pallas import tpu as pltpu
from jax.sharding import PartitionSpec as P

D = 8192
H = 64
KV = 8
HD = 128
STEPS = 4


EPSILON = 1e-06
THETA = 1000000.0
NEGATIVE = -1e30


def rotate(heads, position):
    half = heads.shape[-1] // 2
    freq = THETA ** (-(jnp.arange(half, dtype=jnp.float32) * 2.0 / heads.shape[-1]))
    angle = position.astype(jnp.float32)[:, None, None] * freq[None, None, :]
    cosine = jnp.cos(angle)
    sine = jnp.sin(angle)
    first = heads[..., :half]
    second = heads[..., half:]
    return jnp.concatenate(
        [first * cosine - second * sine, second * cosine + first * sine], axis=-1
    )


MESH = pl.DeviceIdType.MESH


def greet(partners):
    barrier = pltpu.get_barrier_semaphore()
    for partner in partners:
        pl.semaphore_signal(barrier, inc=1, device_id=partner, device_id_type=MESH)
    pl.semaphore_wait(barrier, len(partners))


def remote(src, dst, send, recv, partner):
    return pltpu.make_async_remote_copy(
        src_ref=src,
        dst_ref=dst,
        send_sem=send,
        recv_sem=recv,
        device_id=partner,
        device_id_type=MESH,
    )


def mlp_kernel(
    zs,
    ss,
    width,
    mid_ref,
    norm_ref,
    wg_hbm,
    wu_hbm,
    wd_hbm,
    out_ref,
    wg,
    wu,
    wd,
    cut,
    square,
    got,
    got_sq,
    normed,
    own_g,
    own_u,
    send_r,
    recv_r,
    send_l,
    recv_l,
    hid,
    down,
    parts,
    landed,
    sums,
    back,
    w_sem,
    a_send,
    a_recv,
    b_send,
    b_recv,
    rs_send,
    rs_recv,
    ag_send,
    ag_recv,
    d_send,
    d_recv,
    e_send,
    e_recv,
):
    z = lax.axis_index("req")
    s = lax.axis_index("seq")
    f32 = jnp.float32
    rows = mid_ref.shape[0]
    pieces = mid_ref.shape[1] // zs
    units = wg.shape[0]
    half = zs * rows // 2
    loads = [
        pltpu.make_async_copy(wg_hbm, wg, w_sem.at[0]),
        pltpu.make_async_copy(wu_hbm, wu, w_sem.at[1]),
        pltpu.make_async_copy(wd_hbm, wd, w_sem.at[2]),
    ]
    for load in loads:
        load.start()
    z_partners = [{"req": lax.rem(z + k, zs), "seq": s} for k in range(1, zs)]
    s_partners = [{"req": z, "seq": lax.rem(s + k, ss)} for k in range(1, ss)]

    total = jnp.zeros((8, rows), f32)
    for block in range(zs):
        piece = mid_ref[:, block * pieces : (block + 1) * pieces]
        cut[block] = piece
        value = piece.astype(f32)
        total += lax.dot_general(
            jnp.ones((8, pieces), f32),
            value * value,
            (((1,), (1,)), ((), ())),
            precision=lax.Precision.HIGHEST,
            preferred_element_type=f32,
        )
    square[...] = jnp.zeros_like(square)
    square[:, :rows] = total
    greet(z_partners + s_partners)
    first = []
    for k in range(1, zs):
        to = lax.rem(z + k, zs)
        first.append(
            remote(cut.at[to], got.at[s, z], a_send.at[0, k], a_recv.at[0, k], z_partners[k - 1])
        )
        first.append(
            remote(square, got_sq.at[s, z], a_send.at[1, k], a_recv.at[1, k], z_partners[k - 1])
        )
    for copy in first:
        copy.start()
    got[s, z] = cut[z]
    got_sq[s, z] = square[...]
    for copy in first:
        copy.wait_recv()
    second = []
    for k in range(1, ss):
        second.append(
            remote(got.at[s], got.at[s], b_send.at[0, k], b_recv.at[0, k], s_partners[k - 1])
        )
        second.append(
            remote(got_sq.at[s], got_sq.at[s], b_send.at[1, k], b_recv.at[1, k], s_partners[k - 1])
        )
    for copy in second:
        copy.start()
    for copy in second:
        copy.wait_recv()
    for group in range(zs):
        line = got_sq[0, group]
        for other in range(1, ss):
            line = line + got_sq[other, group]
        spread = lax.dot_general(
            line[:, :rows],
            jnp.full((8, 128), 0.125, f32),
            (((0,), (0,)), ((), ())),
            precision=lax.Precision.HIGHEST,
            preferred_element_type=f32,
        )
        inverse = lax.rsqrt(spread / D + EPSILON)[:, :1]
        for other in range(ss):
            gain = norm_ref[:, other * pieces : (other + 1) * pieces]
            normed[group * rows : (group + 1) * rows, other * pieces : (other + 1) * pieces] = (
                got[other, group].astype(f32) * inverse * gain
            ).astype(jnp.bfloat16)

    starts = list(range(0, units, width))
    count = len(starts)
    sizes = [min(width, units - start) for start in starts]
    padded = [-(-size // 128) * 128 for size in sizes]
    if sizes[-1] != padded[-1]:
        send_r[count - 1] = jnp.zeros_like(send_r[count - 1])
        send_l[count - 1] = jnp.zeros_like(send_l[count - 1])
        hid[count - 1] = jnp.zeros_like(hid[count - 1])
    down[...] = jnp.zeros_like(down)
    loads[0].wait()
    loads[1].wait()

    right = {"req": lax.rem(z + 1, zs), "seq": s}
    left = {"req": lax.rem(z + zs - 1, zs), "seq": s}

    def reduce_copy(way, p):
        src, dst, to = ((send_r, recv_r, right), (send_l, recv_l, left))[way]
        lanes = pl.ds(0, 2 * padded[p])
        return remote(
            src.at[p, :, lanes], dst.at[p, :, lanes], rs_send.at[way, p], rs_recv.at[way, p], to
        )

    def hidden_copy(way, p):
        place = (p, pl.ds(half * (1 - way), half), pl.ds(0, padded[p]))
        return remote(
            hid.at[place],
            hid.at[place],
            ag_send.at[way, p],
            ag_recv.at[way, p],
            (left, right)[way],
        )

    def reduce_step(way, p, place):
        size, pad = sizes[p], padded[p]
        base = half * (1 - way)
        cols = slice(starts[p], starts[p] + size)
        gate = own_g[base : base + half, cols]
        up = own_u[base : base + half, cols]
        if place > 0:
            reduce_copy(way, p).wait_recv()
            came = (recv_r, recv_l)[way]
            gate = gate + came[p, :, :size].astype(f32)
            up = up + came[p, :, pad : pad + size].astype(f32)
        if place < zs - 1:
            goes = (send_r, send_l)[way]
            goes[p, :, :size] = gate.astype(jnp.bfloat16)
            goes[p, :, pad : pad + size] = up.astype(jnp.bfloat16)
            reduce_copy(way, p).start()
        else:
            gate = gate.astype(jnp.bfloat16).astype(f32)
            up = up.astype(jnp.bfloat16).astype(f32)
            hid[p, base : base + half, :size] = (gate / (1.0 + jnp.exp(-gate)) * up).astype(
                jnp.bfloat16
            )
            hidden_copy(way, p).start()

    def down_step(p):
        down[...] += jnp.dot(
            hid[p, :, : sizes[p]],
            wd[starts[p] : starts[p] + sizes[p], :],
            preferred_element_type=f32,
        )

    nt = (((1,), (1,)), ((), ()))
    lag = list(range(2 * zs))
    last = lag[2 * zs - 2]
    for i in range(count + last):
        if i < count:
            cols = slice(starts[i], starts[i] + sizes[i])
            own_g[:, cols] = lax.dot_general(normed[...], wg[cols, :], nt, preferred_element_type=f32)
            own_u[:, cols] = lax.dot_general(normed[...], wu[cols, :], nt, preferred_element_type=f32)
        for zz in range(zs):

            @pl.when(z == zz)
            def _(zz=zz, i=i):
                order = (0, 1) if zz < zs // 2 else (1, 0)
                for way in order:
                    place = zz if way == 0 else zs - 1 - zz
                    p = i - lag[place]
                    if 0 <= p < count:
                        reduce_step(way, p, place)
                for way in order[::-1]:
                    place = zs - 1 - zz if way == 0 else zz
                    p = i - lag[zs - 1 + place]
                    if place > 0 and 0 <= p < count:
                        hidden_copy(way, p).wait_recv()
                        if place < zs - 1:
                            hidden_copy(way, p).start()

        if i == last:
            loads[2].wait()
        if i >= last:
            down_step(i - last)

    for other in range(ss):
        parts[other] = down[:, other * pieces : (other + 1) * pieces].astype(jnp.bfloat16)
    third = []
    for k in range(1, ss):
        to = lax.rem(s + k, ss)
        third.append(
            remote(parts.at[to], landed.at[s], d_send.at[k], d_recv.at[k], s_partners[k - 1])
        )
    for copy in third:
        copy.start()
    landed[s] = parts[s]
    for copy in third:
        copy.wait_recv()
    whole = landed[0].astype(f32)
    for other in range(1, ss):
        whole = whole + landed[other].astype(f32)
    for group in range(zs):
        sums[group] = whole[group * rows : (group + 1) * rows]
    fourth = []
    for k in range(1, zs):
        to = lax.rem(z + k, zs)
        fourth.append(
            remote(sums.at[to], back.at[z], e_send.at[k], e_recv.at[k], z_partners[k - 1])
        )
    for copy in fourth:
        copy.start()
    back[z] = sums[z]
    for copy in fourth:
        copy.wait_recv()
    for block in range(zs):
        cols = slice(block * pieces, (block + 1) * pieces)
        out_ref[:, cols] = (mid_ref[:, cols].astype(f32) + back[block]).astype(jnp.bfloat16)

    for copy in first + second + third + fourth:
        copy.wait_send()
    for way in range(2):
        for p in range(count):

            @pl.when(z != (zs - 1 if way == 0 else 0))
            def _(way=way, p=p):
                reduce_copy(way, p).wait_send()

            @pl.when(z != (0 if way == 0 else zs - 1))
            def _(way=way, p=p):
                hidden_copy(way, p).wait_send()


def mlp(middle, norm, w_gate, w_up, w_down, zs, ss):
    rows, features = middle.shape
    pieces = features // zs
    units, depth = w_gate.shape
    quarter = w_down.shape[1]
    width = 512
    count = -(-units // width)
    everyone = zs * rows
    half = everyone // 2
    bf16, f32 = jnp.bfloat16, jnp.float32
    vmem = pl.BlockSpec(memory_space=pltpu.VMEM)
    hbm = pl.BlockSpec(memory_space=pl.ANY)
    dma = pltpu.SemaphoreType.DMA
    return pl.pallas_call(
        functools.partial(mlp_kernel, zs, ss, width),
        name="mlp",
        out_shape=jax.ShapeDtypeStruct(middle.shape, bf16),
        in_specs=[vmem, vmem, hbm, hbm, hbm],
        out_specs=vmem,
        scratch_shapes=[
            pltpu.VMEM(w_gate.shape, bf16),
            pltpu.VMEM(w_up.shape, bf16),
            pltpu.VMEM(w_down.shape, bf16),
            pltpu.VMEM((zs, rows, pieces), bf16),
            pltpu.VMEM((8, 128), f32),
            pltpu.VMEM((ss, zs, rows, pieces), bf16),
            pltpu.VMEM((ss, zs, 8, 128), f32),
            pltpu.VMEM((everyone, depth), bf16),
            pltpu.VMEM((everyone, units), f32),
            pltpu.VMEM((everyone, units), f32),
            pltpu.VMEM((count, half, 2 * width), bf16),
            pltpu.VMEM((count, half, 2 * width), bf16),
            pltpu.VMEM((count, half, 2 * width), bf16),
            pltpu.VMEM((count, half, 2 * width), bf16),
            pltpu.VMEM((count, everyone, width), bf16),
            pltpu.VMEM((everyone, quarter), f32),
            pltpu.VMEM((ss, everyone, pieces), bf16),
            pltpu.VMEM((ss, everyone, pieces), bf16),
            pltpu.VMEM((zs, rows, pieces), f32),
            pltpu.VMEM((zs, rows, pieces), f32),
            dma((3,)),
            dma((2, zs)),
            dma((2, zs)),
            dma((2, ss)),
            dma((2, ss)),
            dma((2, count)),
            dma((2, count)),
            dma((2, count)),
            dma((2, count)),
            dma((ss,)),
            dma((ss,)),
            dma((zs,)),
            dma((zs,)),
        ],
        compiler_params=pltpu.CompilerParams(
            collective_id=0, has_side_effects=True, vmem_limit_bytes=63 * 2**20
        ),
    )(middle, norm, w_gate, w_up, w_down)


def project_kernel(
    zs,
    ss,
    x_ref,
    norm_ref,
    bias_ref,
    w_hbm,
    out_ref,
    w,
    own,
    got,
    normed,
    sent,
    columns,
    w_sem,
    a_send,
    a_recv,
    b_send,
    b_recv,
):
    z = lax.axis_index("req")
    s = lax.axis_index("seq")
    f32 = jnp.float32
    rows, features = x_ref.shape
    blocks = norm_ref.shape[0]
    pieces = features // blocks
    mine = w.shape[1]
    parts = 4
    depth = D // parts
    loads = [
        pltpu.make_async_copy(
            w_hbm.at[pl.ds(part * depth, depth)], w.at[pl.ds(part * depth, depth)], w_sem.at[part]
        )
        for part in range(parts)
    ]
    for load in loads:
        load.start()
    partners = [{"req": z, "seq": lax.rem(s + k, ss)} for k in range(1, ss)]
    own[...] = x_ref[...]
    greet(partners)
    first = [
        remote(own, got.at[s], a_send.at[k], a_recv.at[k], partners[k - 1]) for k in range(1, ss)
    ]
    for copy in first:
        copy.start()
    got[s] = own[...]
    for copy in first:
        copy.wait_recv()
    total = jnp.zeros((rows, 1), f32)
    for other in range(ss):
        value = got[other].astype(f32)
        total += jnp.sum(value * value, axis=1, keepdims=True)
    inverse = lax.rsqrt(total / D + EPSILON)
    for other in range(ss):
        for block in range(blocks):
            lanes = slice(other * pieces, (other + 1) * pieces)
            base = block * ss * pieces + other * pieces
            value = got[other, :, block * pieces : (block + 1) * pieces].astype(f32)
            normed[:, base : base + pieces] = (
                value * inverse * norm_ref[block : block + 1, lanes]
            ).astype(jnp.bfloat16)
    result = jnp.zeros((rows, mine), f32)
    for part in range(parts):
        loads[part].wait()
        span = slice(part * depth, (part + 1) * depth)
        result += jnp.dot(normed[:, span], w[span, :], preferred_element_type=f32)
    sent[...] = (result + bias_ref[...].astype(f32)).astype(jnp.bfloat16)
    second = [
        remote(sent, columns.at[s], b_send.at[k], b_recv.at[k], partners[k - 1])
        for k in range(1, ss)
    ]
    for copy in second:
        copy.start()
    columns[s] = sent[...]
    for copy in second:
        copy.wait_recv()
    for other in range(ss):
        out_ref[:, other * mine : (other + 1) * mine] = columns[other]
    for copy in first + second:
        copy.wait_send()


def project(x, norm, bias, w, zs, ss):
    rows, features = x.shape
    mine = w.shape[1]
    bf16 = jnp.bfloat16
    vmem = pl.BlockSpec(memory_space=pltpu.VMEM)
    dma = pltpu.SemaphoreType.DMA
    return pl.pallas_call(
        functools.partial(project_kernel, zs, ss),
        name="project",
        out_shape=jax.ShapeDtypeStruct((rows, ss * mine), bf16),
        in_specs=[vmem, vmem, vmem, pl.BlockSpec(memory_space=pl.ANY)],
        out_specs=vmem,
        scratch_shapes=[
            pltpu.VMEM(w.shape, bf16),
            pltpu.VMEM((rows, features), bf16),
            pltpu.VMEM((ss, rows, features), bf16),
            pltpu.VMEM((rows, D), bf16),
            pltpu.VMEM((rows, mine), bf16),
            pltpu.VMEM((ss, rows, mine), bf16),
            dma((4,)),
            dma((ss,)),
            dma((ss,)),
            dma((ss,)),
            dma((ss,)),
        ],
        compiler_params=pltpu.CompilerParams(
            collective_id=1, has_side_effects=True, vmem_limit_bytes=48 * 2**20
        ),
    )(x, norm, bias, w)


def merge_kernel(
    zs,
    ss,
    acc_ref,
    stat_ref,
    x_ref,
    w_hbm,
    out_ref,
    w,
    acc,
    stat,
    got,
    got_stat,
    heads,
    everyone,
    joined,
    w_sem,
    a_send,
    a_recv,
    b_send,
    b_recv,
):
    z = lax.axis_index("req")
    s = lax.axis_index("seq")
    f32 = jnp.float32
    rows = x_ref.shape[0]
    per = H // ss
    parts = 4
    depth = D // parts
    loads = [
        pltpu.make_async_copy(
            w_hbm.at[pl.ds(part * depth, depth)], w.at[pl.ds(part * depth, depth)], w_sem.at[part]
        )
        for part in range(parts)
    ]
    for load in loads:
        load.start()
    partners = [{"req": z, "seq": lax.rem(s + k, ss)} for k in range(1, ss)]
    acc[...] = acc_ref[...]
    stat[...] = stat_ref[...]
    greet(partners)
    first = []
    for k in range(1, ss):
        to = lax.rem(s + k, ss)
        first.append(
            remote(stat.at[to], got_stat.at[s], a_send.at[1, k], a_recv.at[1, k], partners[k - 1])
        )
        first.append(
            remote(acc.at[to], got.at[s], a_send.at[0, k], a_recv.at[0, k], partners[k - 1])
        )
    for copy in first:
        copy.start()
    got[s] = acc[s]
    got_stat[s] = stat[s]
    for copy in first:
        copy.wait_recv()
    lines = per * rows // 128
    best = got_stat[0, :lines]
    for other in range(1, ss):
        best = jnp.maximum(best, got_stat[other, :lines])
    shares = [jnp.exp(got_stat[other, :lines] - best) for other in range(ss)]
    denominator = shares[0] * got_stat[0, lines : 2 * lines]
    for other in range(1, ss):
        denominator = denominator + shares[other] * got_stat[other, lines : 2 * lines]
    tall = jnp.transpose(
        jnp.concatenate([share / denominator for share in shares], axis=0)
    )
    for line in range(lines):
        span = slice(line * 128, (line + 1) * 128)
        value = got[0, span, :] * tall[:, line : line + 1]
        for other in range(1, ss):
            at = other * lines + line
            value = value + got[other, span, :] * tall[:, at : at + 1]
        heads[span, :] = value.astype(jnp.bfloat16)
    second = [
        remote(heads, everyone.at[s], b_send.at[k], b_recv.at[k], partners[k - 1])
        for k in range(1, ss)
    ]
    for copy in second:
        copy.start()
    everyone[s] = heads[...]
    for copy in second:
        copy.wait_recv()
    for other in range(ss):
        for head in range(per):
            base = (other * per + head) * HD
            joined[:, base : base + HD] = everyone[other, head * rows : (head + 1) * rows, :]
    result = x_ref[...].astype(f32)
    for part in range(parts):
        loads[part].wait()
        span = slice(part * depth, (part + 1) * depth)
        result += jnp.dot(joined[:, span], w[span, :], preferred_element_type=f32)
    out_ref[...] = result.astype(jnp.bfloat16)
    for copy in first + second:
        copy.wait_send()


def merge(acc, stat, x, w, zs, ss):
    rows, features = x.shape
    bf16, f32 = jnp.bfloat16, jnp.float32
    vmem = pl.BlockSpec(memory_space=pltpu.VMEM)
    dma = pltpu.SemaphoreType.DMA
    return pl.pallas_call(
        functools.partial(merge_kernel, zs, ss),
        name="merge",
        out_shape=jax.ShapeDtypeStruct((rows, features), bf16),
        in_specs=[vmem, vmem, vmem, pl.BlockSpec(memory_space=pl.ANY)],
        out_specs=vmem,
        scratch_shapes=[
            pltpu.VMEM(w.shape, bf16),
            pltpu.VMEM(acc.shape, f32),
            pltpu.VMEM(stat.shape, f32),
            pltpu.VMEM(acc.shape, f32),
            pltpu.VMEM(stat.shape, f32),
            pltpu.VMEM(acc.shape[1:], bf16),
            pltpu.VMEM(acc.shape, bf16),
            pltpu.VMEM((rows, H * HD), bf16),
            dma((4,)),
            dma((2, ss)),
            dma((2, ss)),
            dma((ss,)),
            dma((ss,)),
        ],
        compiler_params=pltpu.CompilerParams(
            collective_id=2, has_side_effects=True, vmem_limit_bytes=48 * 2**20
        ),
    )(acc, stat, x, w)


def on_device(
    hidden_in,
    cache_lens,
    page_table,
    key_cache,
    value_cache,
    norm_attn,
    w_qkv,
    b_qkv,
    w_out,
    norm_mlp,
    w_gate,
    w_up,
    w_down,
):
    steps, requests, blocks, pieces = hidden_in.shape
    rows = steps * requests
    slots, per_page, _ = key_cache.shape
    group = H // KV
    quarter = D // blocks
    seq = quarter // pieces
    scale = 1.0 / math.sqrt(HD)
    zs = D // w_gate.shape[0]
    fast = (
        pieces % 128 == 0
        and w_qkv.shape[1] % 128 == 0
        and zs == blocks
        and zs % 2 == 0
        and rows <= 128
        and rows % 16 == 0
        and H % seq == 0
        and (H // seq) * rows % 128 == 0
    )
    slot_ids = lax.axis_index("seq") * slots + jnp.arange(slots, dtype=jnp.int32)
    matches = page_table[:, :, None] == slot_ids[None, None, :]
    live = jnp.any(matches, axis=(0, 1))
    owner = jnp.sum(
        jnp.where(matches, jnp.arange(requests, dtype=jnp.int32)[:, None, None], 0), axis=(0, 1)
    )
    logical = jnp.sum(
        jnp.where(matches, jnp.arange(page_table.shape[1], dtype=jnp.int32)[None, :, None], 0),
        axis=(0, 1),
    )
    owned = jnp.logical_and(
        jnp.arange(requests, dtype=jnp.int32)[None, :] == owner[:, None], live[:, None]
    )
    slot_length = jnp.sum(jnp.where(owned, cache_lens[None, :], 0), axis=1)
    positions = logical[:, None] * per_page + jnp.arange(per_page, dtype=jnp.int32)[None, :]

    if fast:
        projected = project(
            hidden_in.reshape(rows, blocks * pieces),
            norm_attn.reshape(blocks, quarter),
            b_qkv.reshape(1, -1),
            w_qkv,
            zs,
            seq,
        )
    else:
        flat = (
            lax.all_gather(hidden_in, "seq", axis=3, tiled=True).reshape(rows, D).astype(jnp.float32)
        )
        normed = (
            flat * lax.rsqrt(jnp.mean(flat * flat, axis=1, keepdims=True) + EPSILON) * norm_attn
        ).astype(jnp.bfloat16)
        columns = (
            jnp.dot(normed, w_qkv, preferred_element_type=jnp.float32) + b_qkv.astype(jnp.float32)
        ).astype(jnp.bfloat16)
        projected = lax.all_gather(columns, "seq", axis=1, tiled=True)
    position = (
        jnp.arange(steps, dtype=jnp.int32)[:, None] + cache_lens[None, :]
    ).reshape(rows)
    rotated = rotate(
        projected[:, : (H + KV) * HD].reshape(rows, H + KV, HD).astype(jnp.float32), position
    ).astype(jnp.bfloat16)
    queries = rotated[:, :H].reshape(steps, requests, KV, group, HD)
    new_keys = rotated[:, H:].reshape(steps, requests, KV * HD)
    new_values = projected[:, (H + KV) * HD :].reshape(steps, requests, KV * HD)
    slot_keys = jnp.take(new_keys, owner, axis=1)
    slot_values = jnp.take(new_values, owner, axis=1)
    for step in range(steps):
        write_here = jnp.logical_and(live[:, None], positions == (slot_length + step)[:, None])[
            :, :, None
        ]
        key_cache = jnp.where(write_here, slot_keys[step][:, None, :], key_cache)
        value_cache = jnp.where(write_here, slot_values[step][:, None, :], value_cache)

    slot_queries = jnp.take(queries, owner, axis=1)
    keys_view = key_cache.reshape(slots, per_page, KV, HD)
    values_view = value_cache.reshape(slots, per_page, KV, HD)
    scores = (
        jnp.einsum("tjkgd,jpkd->jktgp", slot_queries, keys_view, preferred_element_type=jnp.float32)
        * scale
    )
    last = slot_length[:, None] + jnp.arange(steps, dtype=jnp.int32)[None, :]
    valid = jnp.logical_and(
        live[:, None, None], positions[:, None, :] <= last[:, :, None]
    )[:, None, :, None, :]
    masked = jnp.where(valid, scores, NEGATIVE)
    page_max = jnp.max(masked, axis=4)
    weights = jnp.where(valid, jnp.exp(masked - page_max[..., None]), 0.0).astype(jnp.bfloat16)
    page_sum = jnp.sum(weights.astype(jnp.float32), axis=4)
    page_acc = jnp.einsum(
        "jktgp,jpkd->jktgd", weights, values_view, preferred_element_type=jnp.float32
    )
    spread = owned[:, :, None, None, None]
    candidates = jnp.where(spread, page_max[:, None], NEGATIVE)
    top = jnp.max(candidates, axis=0)
    factor = jnp.where(spread, jnp.exp(candidates - top[None]), 0.0)
    total = jnp.sum(factor * page_sum[:, None], axis=0)
    summed = jnp.sum(factor[..., None] * page_acc[:, None], axis=0)
    def by_head(value):
        value = jnp.moveaxis(value, 0, 3)
        value = jnp.swapaxes(value, 1, 2)
        return value.reshape((seq, H // seq, rows) + value.shape[4:])

    if fast:
        stat = jnp.concatenate([by_head(top), by_head(total)], axis=1).reshape(seq, -1, 128)
        middle = merge(
            by_head(summed).reshape(seq, -1, HD),
            stat,
            hidden_in.reshape(rows, blocks * pieces),
            w_out.reshape(H * HD, blocks * pieces),
            zs,
            seq,
        )
    else:
        packed = jnp.concatenate(
            [
                by_head(summed).reshape(seq, -1),
                by_head(top).reshape(seq, -1),
                by_head(total).reshape(seq, -1),
            ],
            axis=1,
        )
        packed = lax.all_to_all(packed, "seq", split_axis=0, concat_axis=0, tiled=True)
        count = (H // seq) * rows
        part_acc = packed[:, : count * HD].reshape(seq, count, HD)
        part_top = packed[:, count * HD : count * (HD + 1)]
        part_sum = packed[:, count * (HD + 1) :]
        best = jnp.max(part_top, axis=0)
        share = jnp.exp(part_top - best[None])
        denominator = jnp.sum(share * part_sum, axis=0)
        numerator = jnp.sum(share[..., None] * part_acc, axis=0)
        heads = (numerator / denominator[:, None]).astype(jnp.bfloat16)
        heads = jnp.swapaxes(heads.reshape(H // seq, rows, HD), 0, 1).reshape(rows, -1)
        attended = lax.all_gather(heads, "seq", axis=1, tiled=True)
        branch_out = jnp.dot(
            attended, w_out.reshape(H * HD, blocks * pieces), preferred_element_type=jnp.float32
        ).reshape(rows, blocks, pieces)
        current = hidden_in.reshape(rows, blocks, pieces).astype(jnp.float32)
        middle = (current + branch_out).astype(jnp.bfloat16)
    if fast:
        gain = lax.dynamic_slice(norm_mlp, (lax.axis_index("req") * quarter,), (quarter,))
        output = mlp(
            middle.reshape(rows, blocks * pieces),
            gain.reshape(1, quarter),
            jnp.swapaxes(w_gate, 0, 1),
            jnp.swapaxes(w_up, 0, 1),
            w_down,
            zs,
            seq,
        )
        return (output.reshape(hidden_in.shape), key_cache, value_cache)
    rows_mid = lax.all_gather(middle, "seq", axis=2, tiled=True).astype(jnp.float32)
    inverse = lax.rsqrt(jnp.mean(rows_mid * rows_mid, axis=(1, 2), keepdims=True) + EPSILON)
    normed_mid = (rows_mid * inverse * norm_mlp.reshape(blocks, quarter)).astype(jnp.bfloat16)
    mine = lax.all_to_all(normed_mid, "req", split_axis=1, concat_axis=0, tiled=True).reshape(
        -1, quarter
    )
    gate_part = jnp.dot(mine, w_gate, preferred_element_type=jnp.float32).astype(jnp.bfloat16)
    up_part = jnp.dot(mine, w_up, preferred_element_type=jnp.float32).astype(jnp.bfloat16)
    gate_sum = lax.psum_scatter(gate_part, "req", scatter_dimension=0, tiled=True)
    up_sum = lax.psum_scatter(up_part, "req", scatter_dimension=0, tiled=True)
    hidden_part = (
        jax.nn.silu(gate_sum.astype(jnp.float32)) * up_sum.astype(jnp.float32)
    ).astype(jnp.bfloat16)
    hidden = lax.all_gather(hidden_part, "req", axis=0, tiled=True)
    down = jnp.dot(hidden, w_down, preferred_element_type=jnp.float32)
    sums = lax.psum_scatter(
        down.reshape(down.shape[0], 1, quarter).astype(jnp.bfloat16),
        "seq",
        scatter_dimension=2,
        tiled=True,
    ).astype(jnp.float32)
    back = lax.all_to_all(sums, "req", split_axis=0, concat_axis=1, tiled=True)
    output = (middle.astype(jnp.float32) + back).astype(jnp.bfloat16)
    return (output.reshape(hidden_in.shape), key_cache, value_cache)


def solution(mesh):
    in_specs = (
        P(None, "req", None, "seq"),
        P("req"),
        P("req", None),
        P(("req", "seq"), None, None),
        P(("req", "seq"), None, None),
        P(),
        P(None, "seq"),
        P("seq"),
        P(None, None, "seq"),
        P(),
        P("req", "seq"),
        P("req", "seq"),
        P("seq", "req"),
    )
    out_specs = (
        P(None, "req", None, "seq"),
        P(("req", "seq"), None, None),
        P(("req", "seq"), None, None),
    )
    return jax.shard_map(
        on_device, mesh=mesh, in_specs=in_specs, out_specs=out_specs, check_vma=False
    )
```
